32 devices in a mesh: cache: 2 (over y), tp: 8 (over z, core), cand: 2 (over x).
Axes of the slice: x: 2, y: 2, z: 4, core: 2. Of those that a mesh axis runs over, the one named last changes fastest.
Arguments:
- prompt_inputs: bfloat16 [1536, 8192], P(('cache', 'cand')), may hold values from -6 to 6
- cand_inputs: bfloat16 [4096, 8192], P(('cache', 'cand'), 'tp'), may hold values from -6 to 6
- norm_gain: float32 [8192], replicated, may hold values from 0.1 to 1.9
- w_query: bfloat16 [8192, 8192], P('cache', 'tp'), may hold values from -0.0625 to 0.0625
- w_key: bfloat16 [8192, 1024], P('cache', 'tp'), may hold values from -0.0625 to 0.0625
- w_value: bfloat16 [8192, 1024], P('cache', 'tp'), may hold values from -0.0625 to 0.0625
- q_bias: float32 [8192], P('tp'), may hold values from -180 to 180
- k_bias: float32 [1024], P('tp'), may hold values from -3 to 8
- v_bias: float32 [1024], P('tp'), may hold values from -4 to 4
- cand_lengths: int32 [16], replicated, may hold values from 32 to 256, as said below
- prefix_ends: int32 [16], replicated, may hold values from 384 to 1536, as said below
Outputs:
- attn_out: bfloat16 [4096, 8192], P(('cache', 'cand'), 'tp')
The draws below stay inside these ranges and needn't reach their ends.
Inputs may be any that keep to these rules, and one draw needn't show every extreme that they name: `cand_lengths`: at least one candidate has 256 tokens. `prefix_ends`: at least one candidate follows the whole prompt.
All inputs are finite; a program needn't handle non-finite values.
Results may differ from the reference program's by a relative error of at most 0.0075.
The reference program's roundings to bfloat16 on the way count: a program that leaves them out, or rounds other values in their place, can miss the bound.
Values may be sent and summed in bfloat16 or wider, within the bound.
A program may use at most 192 MiB of HBM per device.

```python
import jax
import jax.numpy as jnp
from jax import lax

D = 8192
HEADS = 64
KV_HEADS = 8
HEAD = 128
CANDS = 16
CLEN = 256
PROMPT = 1536
CTOK = 4096


def draw_q_bias(key, part):
    drawn = jnp.clip(0.5 * jax.random.normal(key, (HEADS * HEAD,), jnp.float32), -3.0, 3.0)
    return drawn


def draw_k_bias(key, part):
    drawn = jnp.clip(0.5 * jax.random.normal(key, (KV_HEADS * HEAD,), jnp.float32), -3.0, 3.0)
    return drawn


def draw_cand_lengths(key, part):
    lengths = jax.random.randint(key, (CANDS,), CLEN // 8, CLEN + 1)
    chosen = jax.random.randint(jax.random.fold_in(key, 3), (), 0, CANDS)
    return jnp.where(jnp.arange(CANDS) == chosen, CLEN, lengths).astype(jnp.int32)


def draw_prefix_ends(key, part):
    prefixes = jax.random.randint(key, (CANDS,), PROMPT // 4, PROMPT + 1)
    chosen = jax.random.randint(jax.random.fold_in(key, 5), (), 0, CANDS)
    return jnp.where(jnp.arange(CANDS) == chosen, PROMPT, prefixes).astype(jnp.int32)


def shard_levels(rng, shape, pieces, smallest, high):
    def one(dim, parts):
        draws = jax.random.uniform(jax.random.fold_in(jax.random.fold_in(rng, 6), dim), (parts,), jnp.float32, smallest / len(pieces), high / len(pieces))
        return jnp.repeat(jnp.exp(draws), shape[dim] // parts).reshape((-1,) + (1,) * (len(shape) - dim - 1))

    loudness = one(*pieces[0])
    for cut in pieces[1:]:
        loudness = loudness * one(*cut)
    return loudness


def gaussian(stream_key, extent, scale, bound, pieces=(), kind=jnp.bfloat16):
    entries = jax.random.normal(stream_key, extent, jnp.float32) * scale
    if len(pieces) > 0:
        entries = shard_levels(stream_key, extent, pieces, -0.22, 0.18) * entries
    return jnp.clip(entries, min=-bound, max=bound).astype(kind)


def setup_inputs(seed: int = 0) -> dict:
    arg_keys = jax.random.split(jax.random.key(seed), 12)
    return {
        "prompt_inputs": gaussian(arg_keys[0], (PROMPT, D), 1.0, 6.0, ((0, 4),)),
        "cand_inputs": gaussian(arg_keys[1], (CTOK, D), 1.0, 6.0, ((0, 4), (1, 8))),
        "norm_gain": jnp.clip(1.0 + 0.18 * jax.random.normal(arg_keys[2], (D,), jnp.float32), 0.1, 1.9),
        "w_query": gaussian(arg_keys[3], (D, HEADS * HEAD), D ** -0.5, 0.0625, ((0, 2), (1, 8))),
        "w_key": gaussian(arg_keys[4], (D, KV_HEADS * HEAD), D ** -0.5, 0.0625, ((0, 2), (1, 8))),
        "w_value": gaussian(arg_keys[5], (D, KV_HEADS * HEAD), D ** -0.5, 0.0625, ((0, 2), (1, 8))),
        "q_bias": draw_q_bias(jax.random.fold_in(arg_keys[11], 71), 0),
        "k_bias": draw_k_bias(jax.random.fold_in(arg_keys[11], 71), 0),
        "v_bias": gaussian(arg_keys[8], (KV_HEADS * HEAD,), 1.0, 4.0, ((0, 8),), jnp.float32),
        "cand_lengths": draw_cand_lengths(jax.random.fold_in(arg_keys[11], 71), 0),
        "prefix_ends": draw_prefix_ends(jax.random.fold_in(arg_keys[11], 71), 0),
    }


ROPE_THETA = 1000000.0
EPSILON = 1e-06

def rotate(tensor, positions):
    half_size = tensor.shape[-1] // 2
    inverse_freq = jnp.power(ROPE_THETA, -jnp.arange(half_size, dtype=jnp.float32) * 2.0 / tensor.shape[-1])
    angles = positions.astype(jnp.float32)[:, None] * inverse_freq[None, :]
    cosine = jnp.cos(angles)[:, None, :]
    sine_part = jnp.sin(angles)[:, None, :]
    first_half = tensor[..., :half_size]
    second = tensor[..., half_size:]
    return jnp.concatenate([first_half * cosine - second * sine_part, second * cosine + first_half * sine_part], axis=-1)

def rms_rows(inputs, gain_vector):
    widened = inputs.astype(jnp.float32)
    inverse = lax.rsqrt(lax.optimization_barrier(jnp.mean(widened * widened, axis=-1, keepdims=True)) + EPSILON)
    return (widened * inverse * gain_vector).astype(jnp.bfloat16)

def reference(prompt_inputs, cand_inputs, norm_gain, w_query, w_key, w_value, q_bias, k_bias, v_bias, cand_lengths, prefix_ends):
    groups = HEADS // KV_HEADS
    normed_p = rms_rows(prompt_inputs, norm_gain)
    normed_c = rms_rows(cand_inputs, norm_gain)
    prompt_pos = jnp.arange(PROMPT, dtype=jnp.int32)
    cand_rows = jnp.arange(CTOK, dtype=jnp.int32)
    cand_pos = (prefix_ends[cand_rows // CLEN] + cand_rows % CLEN).astype(jnp.int32)

    def keys_of(normed, positions):
        key_part = jnp.dot(normed, w_key, preferred_element_type=jnp.float32) + k_bias
        key_part = rotate(key_part.reshape(-1, KV_HEADS, HEAD), positions).astype(jnp.bfloat16)
        value_part = (jnp.dot(normed, w_value, preferred_element_type=jnp.float32) + v_bias).astype(jnp.bfloat16)
        return (lax.optimization_barrier(key_part), lax.optimization_barrier(value_part.reshape(-1, KV_HEADS, HEAD)))
    keys_p, values_p = keys_of(normed_p, prompt_pos)
    keys_c, values_c = keys_of(normed_c, cand_pos)
    queries = jnp.dot(normed_c, w_query, preferred_element_type=jnp.float32) + q_bias
    queries = rotate(queries.reshape(CTOK, HEADS, HEAD), cand_pos).astype(jnp.bfloat16)
    queries = lax.optimization_barrier(queries).reshape(CANDS, CLEN, KV_HEADS, groups, HEAD)
    keys_c = keys_c.reshape(CANDS, CLEN, KV_HEADS, HEAD)
    values_c = values_c.reshape(CANDS, CLEN, KV_HEADS, HEAD)
    scaling = HEAD ** (-0.5)

    def per_item(item_index):
        cand_index = item_index // KV_HEADS
        head_index = item_index % KV_HEADS
        query_rows = queries[cand_index, :, head_index].astype(jnp.float32)
        key_rows = jnp.concatenate([keys_p[:, head_index], keys_c[cand_index, :, head_index]], 0).astype(jnp.float32)
        value_rows = jnp.concatenate([values_p[:, head_index], values_c[cand_index, :, head_index]], 0).astype(jnp.float32)
        scores = jnp.einsum('rqd,nd->rqn', query_rows, key_rows) * scaling
        key_ids = jnp.arange(PROMPT + CLEN, dtype=jnp.int32)
        row_ids = jnp.arange(CLEN, dtype=jnp.int32)
        visible = jnp.where(key_ids[None, :] < PROMPT, key_ids[None, :] < prefix_ends[cand_index], key_ids[None, :] - PROMPT <= row_ids[:, None])
        scores = jnp.where(visible[:, None, :], scores, -jnp.inf)
        maxima = lax.optimization_barrier(jnp.max(scores, axis=-1, keepdims=True))
        weights = jnp.exp(scores - maxima)
        totals = lax.optimization_barrier(jnp.sum(weights, axis=-1))
        rounded = lax.optimization_barrier(weights.astype(jnp.bfloat16)).astype(jnp.float32)
        output = jnp.einsum('rqn,nd->rqd', rounded, value_rows) / totals[..., None]
        output = jnp.where((row_ids < cand_lengths[cand_index])[:, None, None], output, 0.0)
        return output.astype(jnp.bfloat16)
    results = lax.map(per_item, jnp.arange(CANDS * KV_HEADS, dtype=jnp.int32))
    results = results.reshape(CANDS, KV_HEADS, CLEN, groups, HEAD).transpose(0, 2, 1, 3, 4)
    return results.reshape(CTOK, HEADS * HEAD)
```

```python
import functools
import math

import jax
import jax.numpy as jnp
import numpy as np
from jax import lax
from jax.experimental import pallas as pl
from jax.experimental.pallas import tpu as pltpu
from jax.sharding import PartitionSpec as P

D = 8192
HEADS = 64
KV_HEADS = 8
HEAD = 128
CANDS = 16
CLEN = 256


ROPE_THETA = 1000000.0
EPSILON = 1e-06


def rotate(tensor, positions):
    half_size = tensor.shape[-1] // 2
    inverse_freq = jnp.power(
        ROPE_THETA, -jnp.arange(half_size, dtype=jnp.float32) * 2.0 / tensor.shape[-1]
    )
    angles = positions.astype(jnp.float32)[:, None] * inverse_freq[None, :]
    cosine = jnp.cos(angles)[:, None, :]
    sine_part = jnp.sin(angles)[:, None, :]
    first_half = tensor[..., :half_size]
    second = tensor[..., half_size:]
    return jnp.concatenate(
        [first_half * cosine - second * sine_part, second * cosine + first_half * sine_part],
        axis=-1,
    )


def row_lookup(row_ids, table):
    chosen = (row_ids // CLEN)[:, None] == jnp.arange(CANDS, dtype=jnp.int32)[None, :]
    return jnp.sum(jnp.where(chosen, table[None, :], 0), axis=1)


def attend_kernel(
    prefix_ref, length_ref, offset_ref, q_ref, kvp_ref, kvc_ref, out_ref, *, heads, chunk, scale
):
    cand = pl.program_id(0)
    prefix = prefix_ref[cand]
    length = length_ref[cand]
    offset = offset_ref[cand]
    rows = q_ref.shape[0]
    contract = (((1,), (1,)), ((), ()))

    def scores_of(head, key_rows):
        return (
            lax.dot_general(
                q_ref[:, head * HEAD : (head + 1) * HEAD],
                key_rows,
                contract,
                preferred_element_type=jnp.float32,
            )
            * scale
        )

    def weighted(probabilities, value_rows):
        return jnp.dot(
            probabilities.astype(jnp.bfloat16), value_rows, preferred_element_type=jnp.float32
        )

    own_shape = (rows, kvc_ref.shape[0])
    causal = lax.broadcasted_iota(jnp.int32, own_shape, 1) <= offset + lax.broadcasted_iota(
        jnp.int32, own_shape, 0
    )
    state = []
    for head in range(heads):
        scores = jnp.where(causal, scores_of(head, kvc_ref[:, :HEAD]), -1e30)
        maxima = jnp.max(scores, axis=1, keepdims=True)
        probabilities = jnp.exp2(scores - maxima)
        totals = jnp.sum(probabilities, axis=1, keepdims=True)
        state += [maxima, totals, weighted(probabilities, kvc_ref[:, HEAD:])]

    def advance(turn, running):
        first = pl.multiple_of(turn * chunk, chunk)
        key_rows = kvp_ref[pl.ds(first, chunk), :HEAD]
        value_rows = kvp_ref[pl.ds(first, chunk), HEAD:]
        seen = first + lax.broadcasted_iota(jnp.int32, (rows, chunk), 1) < prefix
        following = []
        for head in range(heads):
            maxima, totals, accumulated = running[3 * head : 3 * head + 3]
            scores = jnp.where(seen, scores_of(head, key_rows), -1e30)
            new_maxima = jnp.maximum(maxima, jnp.max(scores, axis=1, keepdims=True))
            probabilities = jnp.exp2(scores - new_maxima)
            rescale = jnp.exp2(maxima - new_maxima)
            totals = totals * rescale + jnp.sum(probabilities, axis=1, keepdims=True)
            accumulated = accumulated * rescale + weighted(probabilities, value_rows)
            following += [new_maxima, totals, accumulated]
        return tuple(following)

    state = lax.fori_loop(0, (prefix + chunk - 1) // chunk, advance, tuple(state))
    valid = offset + lax.broadcasted_iota(jnp.int32, (rows, HEAD), 0) < length
    for head in range(heads):
        result = state[3 * head + 2] / state[3 * head + 1]
        out_ref[:, head * HEAD : (head + 1) * HEAD] = jnp.where(valid, result, 0.0).astype(
            jnp.bfloat16
        )


def attend(prefixes, lengths, offsets, queries, kv_prompt, kv_cand, kv_local, groups):
    tiles = prefixes.shape[0]
    rows = queries.shape[0] // tiles
    prompt = kv_prompt.shape[0]
    chunk = next(size for size in (512, 256, 128, prompt) if prompt % size == 0)
    heads = 2 if groups % 2 == 0 else 1
    turns = groups // heads
    return pl.pallas_call(
        functools.partial(
            attend_kernel, heads=heads, chunk=chunk, scale=HEAD ** (-0.5) * math.log2(math.e)
        ),
        grid_spec=pltpu.PrefetchScalarGridSpec(
            num_scalar_prefetch=3,
            grid=(tiles, kv_local, turns),
            in_specs=[
                pl.BlockSpec((rows, heads * HEAD), lambda c, k, t, *_: (c, k * turns + t)),
                pl.BlockSpec((prompt, 2 * HEAD), lambda c, k, t, *_: (0, k)),
                pl.BlockSpec((CLEN, 2 * HEAD), lambda c, k, t, *_: (c, k)),
            ],
            out_specs=pl.BlockSpec((rows, heads * HEAD), lambda c, k, t, *_: (c, k * turns + t)),
        ),
        out_shape=jax.ShapeDtypeStruct(queries.shape, jnp.bfloat16),
        cost_estimate=pl.CostEstimate(
            flops=4 * queries.size * (prompt + CLEN),
            bytes_accessed=4 * queries.size,
            transcendentals=queries.size // HEAD * (prompt + CLEN),
        ),
        compiler_params=pltpu.CompilerParams(vmem_limit_bytes=60 * 1024 * 1024),
    )(prefixes, lengths, offsets, queries, kv_prompt, kv_cand)


MESH = pl.DeviceIdType.MESH


def link_orders(depths, chunks):
    orders = [[(0, r) for r in range(chunks)]]
    for depth in range(1, depths):
        ready = {(d + 1, r): k + 2 for k, (d, r) in enumerate(orders[-1])}
        ready.update({(0, r): 0 for r in range(chunks)})
        order = []
        while ready:
            slot = len(order)
            able = [e for e in ready if ready[e] <= slot] or list(ready)
            pick = min(able, key=lambda e: (e[1], e[0]))
            del ready[pick]
            order.append(pick)
        orders.append(order)
    return orders


def project_kernel(
    xc_ref, xp_ref, gain_ref, wq_ref, wk_ref, wv_ref, qb_ref, kb_ref, vb_ref, freq_ref, prefix_ref,
    q_ref, kvc_ref, kvp_ref,
    acts, wts, prompt, cosines, sines, stats,
    load_sem, wsend, wrecv, rsend, rrecv, own_sem, fwd_sem, sib_sem, arr_sem, st_send, st_recv, kp_send, kp_recv,
):
    y, tp, x = lax.axis_index("cache"), lax.axis_index("tp"), lax.axis_index("cand")
    tps = lax.axis_size("tp")
    floors = tps // 2
    z, core = tp // 2, tp % 2
    rows, part = xc_ref.shape
    block = CLEN
    chunks = rows // block
    half = wq_ref.shape[0]
    quarter = half // 2
    piece_rows = quarter // 2
    wide = 2 * HEAD
    columns = wq_ref.shape[1] // wide
    pieces = 2 + 2 * columns
    prompt_rows = xp_ref.shape[0]
    slices = tps
    joined = y * 2 + x

    up, down, sib = (y, tp + 2, x), (y, tp - 2, x), (y, tp + 1 - 2 * core, x)
    over, aside, across = (1 - y, tp, x), (y, tp, 1 - x), (1 - y, tp, 1 - x)
    peers = [(y, (tp + t) % tps, x) for t in range(1, tps)]

    barrier = pltpu.get_barrier_semaphore()
    for peer in peers + [over, aside, across]:
        pl.semaphore_signal(barrier, inc=1, device_id=peer, device_id_type=MESH)

    load_x = pltpu.make_async_copy(xc_ref, acts.at[tp], load_sem.at[0])
    load_p = pltpu.make_async_copy(xp_ref, prompt, load_sem.at[1])
    own_rows = pl.ds(pl.multiple_of(y * half, half), half)
    load_w = [
        pltpu.make_async_copy(wk_ref, wts.at[0, own_rows, :HEAD], load_sem.at[2]),
        pltpu.make_async_copy(wv_ref, wts.at[0, own_rows, HEAD:], load_sem.at[3]),
    ] + [
        pltpu.make_async_copy(
            wq_ref.at[:, j * wide : (j + 1) * wide], wts.at[1 + j, own_rows, :], load_sem.at[4 + j]
        )
        for j in range(columns)
    ]
    load_x.start()
    load_p.start()
    for copy in load_w:
        copy.start()

    def piece_place(i, side_y, side_x):
        base = side_y * half + side_x * quarter
        if i < 2:
            where = pl.ds(pl.multiple_of(base, quarter), quarter)
            return wts.at[0, where, i * HEAD : (i + 1) * HEAD]
        j, h = divmod(i - 2, 2)
        where = pl.ds(pl.multiple_of(base + h * piece_rows, piece_rows), piece_rows)
        return wts.at[1 + j, where, :]

    def direct(i):
        if i < 2:
            src = (wk_ref, wv_ref)[i].at[pl.ds(pl.multiple_of(x * quarter, quarter), quarter), :]
        else:
            j, h = divmod(i - 2, 2)
            where = pl.ds(pl.multiple_of(x * quarter + h * piece_rows, piece_rows), piece_rows)
            src = wq_ref.at[where, j * wide : (j + 1) * wide]
        return pltpu.make_async_remote_copy(
            src_ref=src, dst_ref=piece_place(i, y, x), send_sem=wsend.at[i], recv_sem=wrecv.at[i],
            device_id=over, device_id_type=MESH,
        )

    def relay(i):
        place = piece_place(i, 1 - y, x)
        return pltpu.make_async_remote_copy(
            src_ref=place, dst_ref=place, send_sem=rsend.at[i], recv_sem=rrecv.at[i],
            device_id=aside, device_id_type=MESH,
        )

    def pass_piece(i):
        if 0 <= i < pieces:
            direct(i).wait_recv()
            relay(i).start()

    def send_piece(i):
        if 0 <= i < pieces:
            direct(i).start()

    def slab(s, r):
        return acts.at[s, pl.ds(r * block, block), :]

    def slab_copy(s, r, send, target):
        return pltpu.make_async_remote_copy(
            src_ref=slab(s, r), dst_ref=slab(s, r), send_sem=send, recv_sem=arr_sem.at[s, r],
            device_id=target, device_id_type=MESH,
        )

    def to_sibling(s, r):
        return slab_copy(s, r, sib_sem.at[s, r], sib)

    def forward(s, r, target):
        return slab_copy(s, r, fwd_sem.at[s, r], target)

    def own(r, way):
        return slab_copy(tp, r, own_sem.at[way, r], (up, down)[way])

    orders = link_orders(floors - 1, chunks)
    longest = orders[-1]

    def link_event(k):
        if 0 <= k - 2 < len(longest):
            distance, r = longest[k - 2]

            @pl.when(z == 0)
            def _():
                s = tp + 2 * (distance + 1)
                forward(s, r, down).wait_recv()
                to_sibling(s, r).start()

            @pl.when(z == floors - 1)
            def _():
                s = tp - 2 * (distance + 1)
                forward(s, r, up).wait_recv()
                to_sibling(s, r).start()

        for depth, order in enumerate(orders):
            if k >= len(order):
                continue
            distance, r = order[k]

            def go(way, sign, target):
                if distance == 0:
                    own(r, way).start()
                else:
                    s = tp + sign * 2 * distance
                    copy = forward(s, r, target)
                    copy.wait_recv()
                    copy.start()
                    to_sibling(s, r).start()

            pl.when(z == depth)(functools.partial(go, 0, -1, up))
            pl.when(floors - 1 - z == depth)(functools.partial(go, 1, 1, down))

    load_x.wait()
    for r in range(chunks):
        wide_x = acts[tp, pl.ds(r * block, block), :].astype(jnp.float32)
        squares = wide_x * wide_x
        lanes = squares[:, :HEAD]
        for t in range(1, part // HEAD):
            lanes = lanes + squares[:, t * HEAD : (t + 1) * HEAD]
        for b in range(block // HEAD):
            turned = jnp.transpose(lanes[b * HEAD : (b + 1) * HEAD, :])
            stats[tp, :, pl.ds(r * block + b * HEAD, HEAD)] = jnp.sum(turned, axis=0, keepdims=True)

    pl.semaphore_wait(barrier, tps + 2)

    def stat_copy(t):
        return pltpu.make_async_remote_copy(
            src_ref=stats.at[tp], dst_ref=stats.at[tp], send_sem=st_send.at[t], recv_sem=st_recv.at[tp],
            device_id=peers[t], device_id_type=MESH,
        )

    def stat_arrival(t):
        s = (tp + 1 + t) % tps
        return pltpu.make_async_remote_copy(
            src_ref=stats.at[s], dst_ref=stats.at[s], send_sem=st_send.at[t], recv_sem=st_recv.at[s],
            device_id=peers[t], device_id_type=MESH,
        )

    for t in range(tps - 1):
        stat_copy(t).start()
    for i in range(4):
        send_piece(i)
    for t in range(tps - 1):
        stat_arrival(t).wait_recv()
    total = stats[0]
    for s in range(1, tps):
        total = total + stats[s]
    inverse = lax.rsqrt(total / (part * tps) + EPSILON)

    def start_own(r):
        for way, can in ((0, z < floors - 1), (1, z > 0)):
            pl.when(can)(lambda way=way: own(r, way).start())

    for r in range(chunks):
        line = jnp.broadcast_to(inverse[:, r * block : (r + 1) * block], (HEAD, block))
        column = jnp.concatenate(
            [jnp.transpose(line[:, b * HEAD : (b + 1) * HEAD]) for b in range(block // HEAD)], axis=0
        )
        column = jnp.concatenate([column] * (part // HEAD), axis=1)
        place = (tp, pl.ds(r * block, block), slice(None))
        acts[place] = (acts[place].astype(jnp.float32) * column * gain_ref[tp]).astype(jnp.bfloat16)
        if r == 1:
            link_event(0)
        if r >= 1:
            to_sibling(tp, r - 1).start()
    link_event(1)
    to_sibling(tp, chunks - 1).start()

    lane = lax.broadcasted_iota(jnp.int32, (1, HEAD), 1)
    sign = jnp.where(lane < HEAD // 2, -1.0, 1.0)

    def table(first, count):
        place = first + lax.broadcasted_iota(jnp.int32, (count, HEAD), 0)
        angles = place.astype(jnp.float32) * freq_ref[...]
        return jnp.cos(angles), jnp.sin(angles) * sign

    def fill(b, _):
        start = pl.multiple_of(b * HEAD, HEAD)
        cand = joined * chunks + b // (block // HEAD)
        cosines[pl.ds(start, HEAD), :], sines[pl.ds(start, HEAD), :] = table(
            prefix_ref[cand] + b % (block // HEAD) * HEAD, HEAD
        )
        return 0

    lax.fori_loop(0, rows // HEAD, fill, 0)

    def rotated(value, cosine, sine):
        return value * cosine + pltpu.roll(value, HEAD // 2, 1) * sine

    pass_piece(0)
    link_event(2)
    send_piece(4)

    load_p.wait()
    slab_rows = 32

    def norm_prompt(b, _):
        where = pl.ds(pl.multiple_of(b * slab_rows, slab_rows), slab_rows)
        squares = jnp.zeros((slab_rows, 1), jnp.float32)
        for s in range(slices):
            value = prompt[where, s * part : (s + 1) * part].astype(jnp.float32)
            squares = squares + jnp.sum(value * value, axis=1, keepdims=True)
        scale = lax.rsqrt(squares / (part * slices) + EPSILON)
        for s in range(slices):
            value = prompt[where, s * part : (s + 1) * part].astype(jnp.float32)
            prompt[where, s * part : (s + 1) * part] = (value * scale * gain_ref[s]).astype(jnp.bfloat16)
        return 0

    lax.fori_loop(0, prompt_rows // slab_rows, norm_prompt, 0)
    pass_piece(1)
    link_event(3)
    send_piece(5)
    pass_piece(2)
    link_event(4)

    def await_piece(i):
        place = piece_place(i, 1 - y, 1 - x)
        pltpu.make_async_remote_copy(
            src_ref=place, dst_ref=place, send_sem=rsend.at[i], recv_sem=rrecv.at[i],
            device_id=aside, device_id_type=MESH,
        ).wait_recv()

    load_w[0].wait()
    load_w[1].wait()
    for i in range(2):
        await_piece(i)

    def prompt_block(b, _):
        where = pl.ds(pl.multiple_of(b * HEAD, HEAD), HEAD)
        product = jnp.dot(prompt[where, :part], wts[0, :part, :], preferred_element_type=jnp.float32)
        for s in range(1, slices):
            product = product + jnp.dot(
                prompt[where, s * part : (s + 1) * part],
                wts[0, s * part : (s + 1) * part, :],
                preferred_element_type=jnp.float32,
            )
        cosine, sine = table(joined * prompt_rows + b * HEAD, HEAD)
        kvp_ref[joined, where, :HEAD] = rotated(product[:, :HEAD] + kb_ref[...], cosine, sine).astype(jnp.bfloat16)
        kvp_ref[joined, where, HEAD:] = (product[:, HEAD:] + vb_ref[...]).astype(jnp.bfloat16)
        return 0

    lax.fori_loop(0, prompt_rows // HEAD, prompt_block, 0)

    def prompt_copy(n, slot):
        return pltpu.make_async_remote_copy(
            src_ref=kvp_ref.at[slot], dst_ref=kvp_ref.at[slot], send_sem=kp_send.at[n], recv_sem=kp_recv.at[n],
            device_id=(over, aside, across)[n], device_id_type=MESH,
        )

    for n in range(3):
        prompt_copy(n, joined).start()
    for i in range(6, 8):
        send_piece(i)
    pass_piece(3)
    link_event(5)
    for i in range(8, pieces):
        send_piece(i)

    def await_columns(j):
        load_w[2 + j].wait()
        await_piece(2 + 2 * j)
        await_piece(3 + 2 * j)

    def await_chunk(r):
        for f in range(floors):
            to_sibling(2 * f + 1 - core, r).wait_recv()

    plan = []
    def add(events, *units):
        for n, unit in enumerate(units):
            plan.append((events if n == 0 else [], unit))

    E, P, C, J = link_event, pass_piece, await_chunk, await_columns
    add([(P, 4), (E, 6), (C, 0), (J, 0)], (0, 0), (0, 1))
    add([(P, 5), (E, 7), (C, 1)], (1, 0), (1, 1))
    add([(P, 6), (E, 8), (J, 1)], (0, 2), (1, 2))
    add([(P, 7), (E, 9), (P, 8), (E, 10), (C, 2)], (2, 0), (2, 1), (2, 2))
    add([(P, 9), (J, 2)], (0, 3), (1, 3), (2, 3))
    add([(E, 11), (E, 12), (J, 3)], (0, 4), (1, 4), (2, 4))
    add([(E, 13), (C, 3)], (3, 0), (3, 1), (3, 2), (3, 3), (3, 4))

    def unit(u, _):
        for k, (events, _unit) in enumerate(plan):
            if events:

                @pl.when(u == k)
                def _():
                    for call, argument in events:
                        call(argument)

        r, j = 0, 0
        for k, (_events, (unit_r, unit_j)) in enumerate(plan):
            r = r + jnp.where(u == k, unit_r, 0)
            j = j + jnp.where(u == k, unit_j, 0)
        where = pl.ds(pl.multiple_of(r * block, block), block)
        product = jnp.dot(acts[0, where, :], wts[j, :part, :], preferred_element_type=jnp.float32)
        for s in range(1, slices):
            product = product + jnp.dot(
                acts[s, where, :], wts[j, s * part : (s + 1) * part, :], preferred_element_type=jnp.float32
            )
        cosine, sine = cosines[where, :], sines[where, :]

        @pl.when(j == 0)
        def _():
            kvc_ref[where, :HEAD] = rotated(product[:, :HEAD] + kb_ref[...], cosine, sine).astype(jnp.bfloat16)
            kvc_ref[where, HEAD:] = (product[:, HEAD:] + vb_ref[...]).astype(jnp.bfloat16)

        @pl.when(j > 0)
        def _():
            for h in range(2):
                value = product[:, h * HEAD : (h + 1) * HEAD] + qb_ref[j - 1, :, h * HEAD : (h + 1) * HEAD]
                q_ref[j - 1, where, h * HEAD : (h + 1) * HEAD] = rotated(value, cosine, sine).astype(jnp.bfloat16)

        return 0

    lax.fori_loop(0, len(plan), unit, 0)

    for n, slot in enumerate(((1 - y) * 2 + x, y * 2 + 1 - x, (1 - y) * 2 + 1 - x)):
        prompt_copy(n, slot).wait_recv()
        prompt_copy(n, joined).wait_send()
    for t in range(tps - 1):
        stat_copy(t).wait_send()
    for i in range(pieces):
        direct(i).wait_send()
        relay(i).wait_send()
    for r in range(chunks):
        to_sibling(tp, r).wait_send()
        pl.when(z < floors - 1)(lambda: own(r, 0).wait_send())
        pl.when(z > 0)(lambda: own(r, 1).wait_send())
        for f in range(floors):
            s = 2 * f + core

            @pl.when(z != f)
            def _():
                to_sibling(s, r).wait_send()

            @pl.when((f < z) & (z < floors - 1))
            def _():
                forward(s, r, up).wait_send()

            @pl.when((f > z) & (z > 0))
            def _():
                forward(s, r, down).wait_send()


def fits(prompt_inputs, cand_inputs, w_query, w_key):
    rows, part = cand_inputs.shape
    tps = lax.axis_size("tp")
    return (
        lax.axis_size("cache") == 2
        and lax.axis_size("cand") == 2
        and tps % 2 == 0
        and tps >= 4
        and rows == 4 * CLEN
        and w_key.shape[1] == HEAD
        and w_query.shape[1] == 8 * HEAD
        and part * tps == D
        and prompt_inputs.shape[0] % HEAD == 0
        and prompt_inputs.shape[0] <= 4 * HEAD
        and w_query.shape[0] == 4 * part
    )


def project(prompt_inputs, cand_inputs, norm_gain, w_query, w_key, w_value, q_bias, k_bias, v_bias, prefix_ends):
    rows, part = cand_inputs.shape
    tps = lax.axis_size("tp")
    floors, chunks, wide = tps // 2, rows // CLEN, 2 * HEAD
    columns = w_query.shape[1] // wide
    pieces = 2 + 2 * columns
    prompt_rows = prompt_inputs.shape[0]
    half_freq = ROPE_THETA ** (-np.arange(HEAD // 2, dtype=np.float64) * 2.0 / HEAD)
    freq = jnp.asarray(np.concatenate([half_freq, half_freq]).astype(np.float32).reshape(1, HEAD))
    anywhere = pl.BlockSpec(memory_space=pl.ANY)
    vmem = pl.BlockSpec(memory_space=pltpu.VMEM)
    smem = pl.BlockSpec(memory_space=pltpu.SMEM)
    dma = pltpu.SemaphoreType.DMA
    return pl.pallas_call(
        project_kernel,
        out_shape=(
            jax.ShapeDtypeStruct((columns, rows, wide), jnp.bfloat16),
            jax.ShapeDtypeStruct((rows, wide), jnp.bfloat16),
            jax.ShapeDtypeStruct((4, prompt_rows, wide), jnp.bfloat16),
        ),
        in_specs=[anywhere, anywhere, vmem, anywhere, anywhere, anywhere, vmem, vmem, vmem, vmem, smem],
        out_specs=(vmem, vmem, vmem),
        scratch_shapes=[
            pltpu.VMEM((tps, rows, part), jnp.bfloat16),
            pltpu.VMEM((1 + columns, part * tps, wide), jnp.bfloat16),
            pltpu.VMEM((prompt_rows, part * tps), jnp.bfloat16),
            pltpu.VMEM((rows, HEAD), jnp.float32),
            pltpu.VMEM((rows, HEAD), jnp.float32),
            pltpu.VMEM((tps, 1, rows), jnp.float32),
            dma((4 + columns,)),
            dma((pieces,)),
            dma((pieces,)),
            dma((pieces,)),
            dma((pieces,)),
            dma((2, chunks)),
            dma((tps, chunks)),
            dma((tps, chunks)),
            dma((tps, chunks)),
            dma((tps - 1,)),
            dma((tps,)),
            dma((3,)),
            dma((3,)),
        ],
        compiler_params=pltpu.CompilerParams(
            collective_id=0, has_side_effects=True, vmem_limit_bytes=64 * 1024 * 1024 - 65536
        ),
        name="project",
    )(
        cand_inputs.reshape(rows, part),
        prompt_inputs,
        norm_gain.reshape(tps, 1, part),
        w_query,
        w_key,
        w_value,
        q_bias.reshape(columns, 1, wide),
        k_bias.reshape(1, HEAD),
        v_bias.reshape(1, HEAD),
        freq,
        prefix_ends,
    )


def query_product(normed, w_query):
    caches = lax.axis_size("cache")
    cands = lax.axis_size("cand")
    depth = w_query.shape[0]
    if caches != 2 or cands != 2 or depth % 4 != 0:
        return jnp.dot(
            normed,
            lax.all_gather(w_query, "cache", axis=0, tiled=True),
            preferred_element_type=jnp.float32,
        )
    mine = lax.axis_index("cache")
    side = lax.axis_index("cand")
    part = depth // 4
    swap = [(0, 1), (1, 0)]
    direct = [
        lax.ppermute(
            lax.dynamic_slice_in_dim(w_query, (2 * side + turn) * part, part), "cache", swap
        )
        for turn in range(2)
    ]
    relayed = [lax.ppermute(piece, "cand", swap) for piece in direct]

    def product(first, weights):
        columns = lax.dynamic_slice_in_dim(normed, first, weights.shape[0], 1)
        return jnp.dot(columns, weights, preferred_element_type=jnp.float32)

    total = product(mine * depth, w_query)
    other = (1 - mine) * depth
    for turn in range(2):
        total = total + product(other + (2 * side + turn) * part, direct[turn])
    for turn in range(2):
        total = total + product(other + (2 * (1 - side) + turn) * part, relayed[turn])
    return total


def per_device(
    prompt_inputs,
    cand_inputs,
    norm_gain,
    w_query,
    w_key,
    w_value,
    q_bias,
    k_bias,
    v_bias,
    cand_lengths,
    prefix_ends,
):
    prompt_dev = prompt_inputs.shape[0]
    cand_dev = cand_inputs.shape[0]
    head_size = HEAD
    kv_local = w_key.shape[1] // head_size
    groups = HEADS // KV_HEADS
    kv_width = kv_local * head_size
    joined = lax.axis_index("cache") * lax.axis_size("cand") + lax.axis_index("cand")
    if fits(prompt_inputs, cand_inputs, w_query, w_key):
        q_cand, kv_c, kv_p = project(
            prompt_inputs, cand_inputs, norm_gain, w_query, w_key, w_value, q_bias, k_bias, v_bias, prefix_ends
        )
        tile_first = joined * cand_dev + CLEN * jnp.arange(cand_dev // CLEN, dtype=jnp.int32)
        return attend(
            row_lookup(tile_first, prefix_ends),
            row_lookup(tile_first, cand_lengths),
            tile_first % CLEN,
            q_cand.transpose(1, 0, 2).reshape(cand_dev, -1),
            kv_p.reshape(-1, 2 * kv_width),
            kv_c,
            kv_local,
            groups,
        )
    widened_p = prompt_inputs.astype(jnp.float32)
    normed_p = (
        widened_p
        * lax.rsqrt(jnp.mean(widened_p * widened_p, axis=-1, keepdims=True) + EPSILON)
        * norm_gain
    ).astype(jnp.bfloat16)
    widened_c = cand_inputs.astype(jnp.float32)
    squares = lax.psum(jnp.sum(widened_c * widened_c, axis=-1), "tp")
    part_width = cand_inputs.shape[1]
    gain_part = lax.dynamic_slice_in_dim(norm_gain, lax.axis_index("tp") * part_width, part_width)
    normed_part = (widened_c * lax.rsqrt(squares / D + EPSILON)[:, None] * gain_part).astype(
        jnp.bfloat16
    )
    normed_c = lax.all_gather(normed_part, "tp", axis=1, tiled=True)
    row_ids = joined * cand_dev + jnp.arange(cand_dev, dtype=jnp.int32)
    prefix_row = row_lookup(row_ids, prefix_ends)
    cand_pos = prefix_row + row_ids % CLEN
    prompt_pos = joined * prompt_dev + jnp.arange(prompt_dev, dtype=jnp.int32)
    key_value = jnp.concatenate([w_key, w_value], axis=1)
    if lax.axis_size("cache") == 2:
        other_half = lax.ppermute(key_value, "cache", [(0, 1), (1, 0)])
        key_value = jnp.where(
            lax.axis_index("cache") == 0,
            jnp.concatenate([key_value, other_half], axis=0),
            jnp.concatenate([other_half, key_value], axis=0),
        )
    else:
        key_value = lax.all_gather(key_value, "cache", axis=0, tiled=True)
    kv_prompt = jnp.dot(normed_p, key_value, preferred_element_type=jnp.float32)

    def keys_values(product, positions):
        rows = product.shape[0]
        keys = rotate(
            (product[:, :kv_width] + k_bias).reshape(rows, kv_local, head_size), positions
        ).astype(jnp.bfloat16)
        values = (product[:, kv_width:] + v_bias).astype(jnp.bfloat16)
        values = values.reshape(rows, kv_local, head_size)
        return jnp.concatenate([keys, values], axis=2).reshape(rows, 2 * kv_width)

    kv_p = lax.all_gather(
        keys_values(kv_prompt, prompt_pos), ("cache", "cand"), axis=0, tiled=True
    )
    q_cand = query_product(normed_c, w_query)
    kv_c = keys_values(jnp.dot(normed_c, key_value, preferred_element_type=jnp.float32), cand_pos)
    queries = rotate(
        (q_cand + q_bias).reshape(cand_dev, kv_local * groups, head_size), cand_pos
    ).astype(jnp.bfloat16)
    tile_rows = min(cand_dev, CLEN)
    tile_first = joined * cand_dev + tile_rows * jnp.arange(cand_dev // tile_rows, dtype=jnp.int32)
    prefixes = row_lookup(tile_first, prefix_ends)
    lengths = row_lookup(tile_first, cand_lengths)
    offsets = tile_first % CLEN
    if cand_dev < CLEN:
        kv_c = lax.all_gather(kv_c, ("cache", "cand"), axis=0, tiled=True)
        kv_c = lax.dynamic_slice_in_dim(kv_c, joined * cand_dev // CLEN * CLEN, CLEN)
    return attend(
        prefixes,
        lengths,
        offsets,
        queries.reshape(cand_dev, kv_local * groups * head_size),
        kv_p,
        kv_c,
        kv_local,
        groups,
    )


def solution(mesh):
    placed = (
        P(("cache", "cand"), None),
        P(("cache", "cand"), "tp"),
        P(),
        P("cache", "tp"),
        P("cache", "tp"),
        P("cache", "tp"),
        P("tp"),
        P("tp"),
        P("tp"),
        P(),
        P(),
    )
    return jax.shard_map(
        per_device,
        mesh=mesh,
        in_specs=placed,
        out_specs=P(("cache", "cand"), "tp"),
        check_vma=False,
    )
```

```python
import functools
import math

import jax
import jax.numpy as jnp
import numpy as np
from jax import lax
from jax.experimental import pallas as pl
from jax.experimental.pallas import tpu as pltpu
from jax.sharding import PartitionSpec as P

D = 8192
HEADS = 64
KV_HEADS = 8
HEAD = 128
CANDS = 16
CLEN = 256


ROPE_THETA = 1000000.0
EPSILON = 1e-06


def rotate(tensor, positions):
    half_size = tensor.shape[-1] // 2
    inverse_freq = jnp.power(
        ROPE_THETA, -jnp.arange(half_size, dtype=jnp.float32) * 2.0 / tensor.shape[-1]
    )
    angles = positions.astype(jnp.float32)[:, None] * inverse_freq[None, :]
    cosine = jnp.cos(angles)[:, None, :]
    sine_part = jnp.sin(angles)[:, None, :]
    first_half = tensor[..., :half_size]
    second = tensor[..., half_size:]
    return jnp.concatenate(
        [first_half * cosine - second * sine_part, second * cosine + first_half * sine_part],
        axis=-1,
    )


def row_lookup(row_ids, table):
    chosen = (row_ids // CLEN)[:, None] == jnp.arange(CANDS, dtype=jnp.int32)[None, :]
    return jnp.sum(jnp.where(chosen, table[None, :], 0), axis=1)


def attend_kernel(
    prefix_ref, length_ref, offset_ref, q_ref, kvp_ref, kvc_ref, out_ref, *, heads, chunk, scale
):
    cand = pl.program_id(0)
    prefix = prefix_ref[cand]
    length = length_ref[cand]
    offset = offset_ref[cand]
    rows = q_ref.shape[0]
    contract = (((1,), (1,)), ((), ()))

    def scores_of(head, key_rows):
        return (
            lax.dot_general(
                q_ref[:, head * HEAD : (head + 1) * HEAD],
                key_rows,
                contract,
                preferred_element_type=jnp.float32,
            )
            * scale
        )

    def weighted(probabilities, value_rows):
        return jnp.dot(
            probabilities.astype(jnp.bfloat16), value_rows, preferred_element_type=jnp.float32
        )

    own_shape = (rows, kvc_ref.shape[0])
    causal = lax.broadcasted_iota(jnp.int32, own_shape, 1) <= offset + lax.broadcasted_iota(
        jnp.int32, own_shape, 0
    )
    state = []
    for head in range(heads):
        scores = jnp.where(causal, scores_of(head, kvc_ref[:, :HEAD]), -1e30)
        maxima = jnp.max(scores, axis=1, keepdims=True)
        probabilities = jnp.exp2(scores - maxima)
        totals = jnp.sum(probabilities, axis=1, keepdims=True)
        state += [maxima, totals, weighted(probabilities, kvc_ref[:, HEAD:])]

    def advance(turn, running):
        first = pl.multiple_of(turn * chunk, chunk)
        key_rows = kvp_ref[pl.ds(first, chunk), :HEAD]
        value_rows = kvp_ref[pl.ds(first, chunk), HEAD:]
        seen = first + lax.broadcasted_iota(jnp.int32, (rows, chunk), 1) < prefix
        following = []
        for head in range(heads):
            maxima, totals, accumulated = running[3 * head : 3 * head + 3]
            scores = jnp.where(seen, scores_of(head, key_rows), -1e30)
            new_maxima = jnp.maximum(maxima, jnp.max(scores, axis=1, keepdims=True))
            probabilities = jnp.exp2(scores - new_maxima)
            rescale = jnp.exp2(maxima - new_maxima)
            totals = totals * rescale + jnp.sum(probabilities, axis=1, keepdims=True)
            accumulated = accumulated * rescale + weighted(probabilities, value_rows)
            following += [new_maxima, totals, accumulated]
        return tuple(following)

    state = lax.fori_loop(0, (prefix + chunk - 1) // chunk, advance, tuple(state))
    valid = offset + lax.broadcasted_iota(jnp.int32, (rows, HEAD), 0) < length
    for head in range(heads):
        result = state[3 * head + 2] / state[3 * head + 1]
        out_ref[:, head * HEAD : (head + 1) * HEAD] = jnp.where(valid, result, 0.0).astype(
            jnp.bfloat16
        )


def attend(prefixes, lengths, offsets, queries, kv_prompt, kv_cand, kv_local, groups):
    tiles = prefixes.shape[0]
    rows = queries.shape[0] // tiles
    prompt = kv_prompt.shape[0]
    chunk = next(size for size in (512, 256, 128, prompt) if prompt % size == 0)
    heads = 2 if groups % 2 == 0 else 1
    turns = groups // heads
    return pl.pallas_call(
        functools.partial(
            attend_kernel, heads=heads, chunk=chunk, scale=HEAD ** (-0.5) * math.log2(math.e)
        ),
        grid_spec=pltpu.PrefetchScalarGridSpec(
            num_scalar_prefetch=3,
            grid=(tiles, kv_local, turns),
            in_specs=[
                pl.BlockSpec((rows, heads * HEAD), lambda c, k, t, *_: (c, k * turns + t)),
                pl.BlockSpec((prompt, 2 * HEAD), lambda c, k, t, *_: (0, k)),
                pl.BlockSpec((CLEN, 2 * HEAD), lambda c, k, t, *_: (c, k)),
            ],
            out_specs=pl.BlockSpec((rows, heads * HEAD), lambda c, k, t, *_: (c, k * turns + t)),
        ),
        out_shape=jax.ShapeDtypeStruct(queries.shape, jnp.bfloat16),
        cost_estimate=pl.CostEstimate(
            flops=4 * queries.size * (prompt + CLEN),
            bytes_accessed=4 * queries.size,
            transcendentals=queries.size // HEAD * (prompt + CLEN),
        ),
        compiler_params=pltpu.CompilerParams(vmem_limit_bytes=60 * 1024 * 1024),
    )(prefixes, lengths, offsets, queries, kv_prompt, kv_cand)


MESH = pl.DeviceIdType.MESH


def link_orders(depths, chunks):
    orders = [[(0, r) for r in range(chunks)]]
    for depth in range(1, depths):
        ready = {(d + 1, r): k + 2 for k, (d, r) in enumerate(orders[-1])}
        ready.update({(0, r): 0 for r in range(chunks)})
        order = []
        while ready:
            slot = len(order)
            able = [e for e in ready if ready[e] <= slot] or list(ready)
            pick = min(able, key=lambda e: (e[1], e[0]))
            del ready[pick]
            order.append(pick)
        orders.append(order)
    return orders


def layer_kernel(
    xc_ref, xp_ref, gain_ref, wq_ref, wk_ref, wv_ref, qb_ref, kb_ref, vb_ref, freq_ref, prefix_ref, length_ref,
    out_ref,
    acts, wts, prompt, cosines, sines, stats, keys_p, values_p, keys_c, values_c, hidden, scores, results,
    load_sem, wsend, wrecv, rsend, rrecv, own_sem, fwd_sem, sib_sem, arr_sem, st_send, st_recv, kp_send, kp_recv, out_sem,
):
    y, tp, x = lax.axis_index("cache"), lax.axis_index("tp"), lax.axis_index("cand")
    tps = lax.axis_size("tp")
    floors = tps // 2
    z, core = tp // 2, tp % 2
    rows, part = xc_ref.shape
    block = CLEN
    chunks = rows // block
    half = wq_ref.shape[0]
    quarter = half // 2
    piece_rows = quarter // 2
    wide = 2 * HEAD
    columns = wq_ref.shape[1] // wide
    pieces = 2 + 2 * columns
    prompt_rows = xp_ref.shape[0]
    slices = tps
    joined = y * 2 + x

    up, down, sib = (y, tp + 2, x), (y, tp - 2, x), (y, tp + 1 - 2 * core, x)
    over, aside, across = (1 - y, tp, x), (y, tp, 1 - x), (1 - y, tp, 1 - x)
    peers = [(y, (tp + t) % tps, x) for t in range(1, tps)]

    barrier = pltpu.get_barrier_semaphore()
    for peer in peers + [over, aside, across]:
        pl.semaphore_signal(barrier, inc=1, device_id=peer, device_id_type=MESH)

    load_x = pltpu.make_async_copy(xc_ref, acts.at[tp], load_sem.at[0])
    load_p = pltpu.make_async_copy(xp_ref, prompt, load_sem.at[1])
    own_rows = pl.ds(pl.multiple_of(y * half, half), half)
    load_w = [
        pltpu.make_async_copy(wk_ref, wts.at[0, own_rows, :HEAD], load_sem.at[2]),
        pltpu.make_async_copy(wv_ref, wts.at[0, own_rows, HEAD:], load_sem.at[3]),
    ] + [
        pltpu.make_async_copy(
            wq_ref.at[:, j * wide : (j + 1) * wide], wts.at[1 + j, own_rows, :], load_sem.at[4 + j]
        )
        for j in range(columns)
    ]
    load_x.start()
    load_p.start()
    for copy in load_w:
        copy.start()

    def piece_place(i, side_y, side_x):
        base = side_y * half + side_x * quarter
        if i < 2:
            where = pl.ds(pl.multiple_of(base, quarter), quarter)
            return wts.at[0, where, i * HEAD : (i + 1) * HEAD]
        j, h = divmod(i - 2, 2)
        where = pl.ds(pl.multiple_of(base + h * piece_rows, piece_rows), piece_rows)
        return wts.at[1 + j, where, :]

    def direct(i):
        if i < 2:
            src = (wk_ref, wv_ref)[i].at[pl.ds(pl.multiple_of(x * quarter, quarter), quarter), :]
        else:
            j, h = divmod(i - 2, 2)
            where = pl.ds(pl.multiple_of(x * quarter + h * piece_rows, piece_rows), piece_rows)
            src = wq_ref.at[where, j * wide : (j + 1) * wide]
        return pltpu.make_async_remote_copy(
            src_ref=src, dst_ref=piece_place(i, y, x), send_sem=wsend.at[i], recv_sem=wrecv.at[i],
            device_id=over, device_id_type=MESH,
        )

    def relay(i):
        place = piece_place(i, 1 - y, x)
        return pltpu.make_async_remote_copy(
            src_ref=place, dst_ref=place, send_sem=rsend.at[i], recv_sem=rrecv.at[i],
            device_id=aside, device_id_type=MESH,
        )

    def pass_piece(i):
        if 0 <= i < pieces:
            direct(i).wait_recv()
            relay(i).start()

    def send_piece(i):
        if 0 <= i < pieces:
            direct(i).start()

    def slab(s, r):
        return acts.at[s, pl.ds(r * block, block), :]

    def slab_copy(s, r, send, target):
        return pltpu.make_async_remote_copy(
            src_ref=slab(s, r), dst_ref=slab(s, r), send_sem=send, recv_sem=arr_sem.at[s, r],
            device_id=target, device_id_type=MESH,
        )

    def to_sibling(s, r):
        return slab_copy(s, r, sib_sem.at[s, r], sib)

    def forward(s, r, target):
        return slab_copy(s, r, fwd_sem.at[s, r], target)

    def own(r, way):
        return slab_copy(tp, r, own_sem.at[way, r], (up, down)[way])

    orders = link_orders(floors - 1, chunks)
    longest = orders[-1]

    def link_event(k):
        if 0 <= k - 2 < len(longest):
            distance, r = longest[k - 2]

            @pl.when(z == 0)
            def _():
                s = tp + 2 * (distance + 1)
                forward(s, r, down).wait_recv()
                to_sibling(s, r).start()

            @pl.when(z == floors - 1)
            def _():
                s = tp - 2 * (distance + 1)
                forward(s, r, up).wait_recv()
                to_sibling(s, r).start()

        for depth, order in enumerate(orders):
            if k >= len(order):
                continue
            distance, r = order[k]

            def go(way, sign, target):
                if distance == 0:
                    own(r, way).start()
                else:
                    s = tp + sign * 2 * distance
                    copy = forward(s, r, target)
                    copy.wait_recv()
                    copy.start()
                    to_sibling(s, r).start()

            pl.when(z == depth)(functools.partial(go, 0, -1, up))
            pl.when(floors - 1 - z == depth)(functools.partial(go, 1, 1, down))

    load_x.wait()
    for r in range(chunks):
        wide_x = acts[tp, pl.ds(r * block, block), :].astype(jnp.float32)
        squares = wide_x * wide_x
        lanes = squares[:, :HEAD]
        for t in range(1, part // HEAD):
            lanes = lanes + squares[:, t * HEAD : (t + 1) * HEAD]
        for b in range(block // HEAD):
            turned = jnp.transpose(lanes[b * HEAD : (b + 1) * HEAD, :])
            stats[tp, :, pl.ds(r * block + b * HEAD, HEAD)] = jnp.sum(turned, axis=0, keepdims=True)

    pl.semaphore_wait(barrier, tps + 2)

    def stat_copy(t):
        return pltpu.make_async_remote_copy(
            src_ref=stats.at[tp], dst_ref=stats.at[tp], send_sem=st_send.at[t], recv_sem=st_recv.at[tp],
            device_id=peers[t], device_id_type=MESH,
        )

    def stat_arrival(t):
        s = (tp + 1 + t) % tps
        return pltpu.make_async_remote_copy(
            src_ref=stats.at[s], dst_ref=stats.at[s], send_sem=st_send.at[t], recv_sem=st_recv.at[s],
            device_id=peers[t], device_id_type=MESH,
        )

    for t in range(tps - 1):
        stat_copy(t).start()
    for i in range(4):
        send_piece(i)
    for t in range(tps - 1):
        stat_arrival(t).wait_recv()
    total = stats[0]
    for s in range(1, tps):
        total = total + stats[s]
    inverse = lax.rsqrt(total / (part * tps) + EPSILON)

    def start_own(r):
        for way, can in ((0, z < floors - 1), (1, z > 0)):
            pl.when(can)(lambda way=way: own(r, way).start())

    for r in range(chunks):
        line = jnp.broadcast_to(inverse[:, r * block : (r + 1) * block], (HEAD, block))
        column = jnp.concatenate(
            [jnp.transpose(line[:, b * HEAD : (b + 1) * HEAD]) for b in range(block // HEAD)], axis=0
        )
        column = jnp.concatenate([column] * (part // HEAD), axis=1)
        place = (tp, pl.ds(r * block, block), slice(None))
        acts[place] = (acts[place].astype(jnp.float32) * column * gain_ref[tp]).astype(jnp.bfloat16)
        if r == 1:
            link_event(0)
        if r >= 1:
            to_sibling(tp, r - 1).start()
    link_event(1)
    to_sibling(tp, chunks - 1).start()

    lane = lax.broadcasted_iota(jnp.int32, (1, HEAD), 1)
    sign = jnp.where(lane < HEAD // 2, -1.0, 1.0)

    def table(first, count):
        place = first + lax.broadcasted_iota(jnp.int32, (count, HEAD), 0)
        angles = place.astype(jnp.float32) * freq_ref[...]
        return jnp.cos(angles), jnp.sin(angles) * sign

    def fill(b, _):
        start = pl.multiple_of(b * HEAD, HEAD)
        cand = joined * chunks + b // (block // HEAD)
        cosines[pl.ds(start, HEAD), :], sines[pl.ds(start, HEAD), :] = table(
            prefix_ref[cand] + b % (block // HEAD) * HEAD, HEAD
        )
        return 0

    lax.fori_loop(0, rows // HEAD, fill, 0)

    def hide(n, _):
        r, b = n // 4, n % 4
        key = b * prompt_rows + lax.broadcasted_iota(jnp.int32, (prompt_rows, HEAD), 0)
        first = lax.broadcasted_iota(jnp.int32, (prompt_rows, HEAD), 1) == 0
        unseen = first & (key >= prefix_ref[joined * chunks + r])
        hidden[r, b] = jnp.where(unseen, -1e30, 0.0).astype(jnp.bfloat16)
        return 0

    lax.fori_loop(0, 4 * chunks, hide, 0)

    def rotated(value, cosine, sine):
        return value * cosine + pltpu.roll(value, HEAD // 2, 1) * sine

    pass_piece(0)
    link_event(2)
    send_piece(4)

    load_p.wait()
    slab_rows = 32

    def norm_prompt(b, _):
        where = pl.ds(pl.multiple_of(b * slab_rows, slab_rows), slab_rows)
        squares = jnp.zeros((slab_rows, 1), jnp.float32)
        for s in range(slices):
            value = prompt[where, s * part : (s + 1) * part].astype(jnp.float32)
            squares = squares + jnp.sum(value * value, axis=1, keepdims=True)
        scale = lax.rsqrt(squares / (part * slices) + EPSILON)
        for s in range(slices):
            value = prompt[where, s * part : (s + 1) * part].astype(jnp.float32)
            prompt[where, s * part : (s + 1) * part] = (value * scale * gain_ref[s]).astype(jnp.bfloat16)
        return 0

    lax.fori_loop(0, prompt_rows // slab_rows, norm_prompt, 0)
    pass_piece(1)
    link_event(3)
    send_piece(5)
    pass_piece(2)
    link_event(4)

    def await_piece(i):
        place = piece_place(i, 1 - y, 1 - x)
        pltpu.make_async_remote_copy(
            src_ref=place, dst_ref=place, send_sem=rsend.at[i], recv_sem=rrecv.at[i],
            device_id=aside, device_id_type=MESH,
        ).wait_recv()

    load_w[0].wait()
    load_w[1].wait()
    for i in range(2):
        await_piece(i)

    def prompt_block(b, _):
        where = pl.ds(pl.multiple_of(b * HEAD, HEAD), HEAD)
        product = jnp.dot(prompt[where, :part], wts[0, :part, :], preferred_element_type=jnp.float32)
        for s in range(1, slices):
            product = product + jnp.dot(
                prompt[where, s * part : (s + 1) * part],
                wts[0, s * part : (s + 1) * part, :],
                preferred_element_type=jnp.float32,
            )
        cosine, sine = table(joined * prompt_rows + b * HEAD, HEAD)
        keys_p[joined, where, :] = rotated(product[:, :HEAD] + kb_ref[...], cosine, sine).astype(jnp.bfloat16)
        values_p[joined, :, where] = jnp.transpose(product[:, HEAD:] + vb_ref[...]).astype(jnp.bfloat16)
        return 0

    lax.fori_loop(0, prompt_rows // HEAD, prompt_block, 0)

    def prompt_copy(n, kind, slot):
        place = (keys_p, values_p)[kind].at[slot]
        return pltpu.make_async_remote_copy(
            src_ref=place, dst_ref=place, send_sem=kp_send.at[n, kind], recv_sem=kp_recv.at[n, kind],
            device_id=(over, aside, across)[n], device_id_type=MESH,
        )

    for n in range(3):
        for kind in range(2):
            prompt_copy(n, kind, joined).start()
    for i in range(6, 8):
        send_piece(i)
    pass_piece(3)
    link_event(5)
    for i in range(8, pieces):
        send_piece(i)

    def await_columns(j):
        load_w[2 + j].wait()
        await_piece(2 + 2 * j)
        await_piece(3 + 2 * j)

    def await_chunk(r):
        for f in range(floors):
            to_sibling(2 * f + 1 - core, r).wait_recv()

    def await_prompt(_):
        for n, slot in enumerate(((1 - y) * 2 + x, y * 2 + 1 - x, (1 - y) * 2 + 1 - x)):
            for kind in range(2):
                prompt_copy(n, kind, slot).wait_recv()

    def result_copy(r, j):
        where = pl.ds(pl.multiple_of(r * block, block), block)
        across_columns = pl.ds(pl.multiple_of(j * wide, wide), wide)
        return pltpu.make_async_copy(
            results.at[j, where, :], out_ref.at[where, across_columns], out_sem.at[r, j]
        )

    def attend_heads(r, queries, write):
        extra = jnp.where(lax.broadcasted_iota(jnp.int32, (block, HEAD), 1) == 0, 1.0, 0.0).astype(jnp.bfloat16)
        own_keys = pl.ds(pl.multiple_of(r * block, block), block)
        contract = (((1,), (1,)), ((), ()))
        states = [{} for _ in queries]
        factor = HEAD ** (-0.5) * math.log2(math.e)

        def span(b):
            return slice(b * prompt_rows, (b + 1) * prompt_rows if b < 4 else 4 * prompt_rows + block)

        def score(h, b):
            state = states[h]
            if b < 4:
                found = lax.dot_general(
                    jnp.concatenate([keys_p[b], hidden[r, b]], axis=1),
                    jnp.concatenate([queries[h], extra], axis=1),
                    contract,
                    preferred_element_type=jnp.float32,
                )
            else:
                found = lax.dot_general(
                    keys_c[own_keys, :], queries[h], contract, preferred_element_type=jnp.float32
                )
                shape = (block, block)
                found = jnp.where(
                    lax.broadcasted_iota(jnp.int32, shape, 0) <= lax.broadcasted_iota(jnp.int32, shape, 1), found, -1e30
                )
            scores[h, span(b), :] = found
            highest = jnp.max(found.reshape(-1, 8, block), axis=0)
            state["max"] = jnp.maximum(state["max"], highest) if "max" in state else highest
            if b == 4:
                state["max"] = jnp.max(state["max"], axis=0, keepdims=True) * factor

        def weigh(h, b):
            state = states[h]
            chances = jnp.exp2(scores[h, span(b), :] * factor - state["max"])
            total = jnp.sum(chances.reshape(-1, 8, block), axis=0)
            values = values_p[b] if b < 4 else values_c[:, own_keys]
            mixed = jnp.dot(values, chances.astype(jnp.bfloat16), preferred_element_type=jnp.float32)
            state["sum"] = state["sum"] + total if "sum" in state else total
            state["mix"] = state["mix"] + mixed if "mix" in state else mixed

        def finish(h):
            state = states[h]
            result = jnp.transpose(state["mix"] / jnp.sum(state["sum"], axis=0, keepdims=True))
            valid = lax.broadcasted_iota(jnp.int32, (block, HEAD), 0) < length_ref[joined * chunks + r]
            write(h, jnp.where(valid, result, 0.0).astype(jnp.bfloat16))

        for b in range(5):
            score(0, b)
        for b in range(5):
            weigh(0, b)
            score(1, b)
        finish(0)
        for b in range(5):
            weigh(1, b)
        finish(1)

    plan = []
    def add(events, *units):
        for n, unit in enumerate(units):
            plan.append((events if n == 0 else [], unit))

    E, P, C, J = link_event, pass_piece, await_chunk, await_columns
    add([(P, 4), (E, 6), (C, 0), (J, 0), (await_prompt, 0)], (0, 0), (0, 1))
    add([(P, 5), (E, 7), (C, 1)], (1, 0), (1, 1))
    add([(P, 6), (E, 8), (J, 1)], (0, 2), (1, 2))
    add([(P, 7), (E, 9), (P, 8), (E, 10), (C, 2)], (2, 0), (2, 1), (2, 2))
    add([(P, 9), (J, 2)], (0, 3), (1, 3), (2, 3))
    add([(E, 11), (E, 12), (J, 3)], (0, 4), (1, 4), (2, 4))
    add([(E, 13), (C, 3)], (3, 0), (3, 1), (3, 2), (3, 3), (3, 4))

    def unit(u, _):
        for k, (events, _unit) in enumerate(plan):
            if events:

                @pl.when(u == k)
                def _():
                    for call, argument in events:
                        call(argument)

        r, j = 0, 0
        for k, (_events, (unit_r, unit_j)) in enumerate(plan):
            r = r + jnp.where(u == k, unit_r, 0)
            j = j + jnp.where(u == k, unit_j, 0)
        where = pl.ds(pl.multiple_of(r * block, block), block)
        product = jnp.dot(acts[0, where, :], wts[j, :part, :], preferred_element_type=jnp.float32)
        for s in range(1, slices):
            product = product + jnp.dot(
                acts[s, where, :], wts[j, s * part : (s + 1) * part, :], preferred_element_type=jnp.float32
            )
        cosine, sine = cosines[where, :], sines[where, :]

        @pl.when(j == 0)
        def _():
            keys_c[where, :] = rotated(product[:, :HEAD] + kb_ref[...], cosine, sine).astype(jnp.bfloat16)
            turned = product[:, HEAD:] + vb_ref[...]
            for b in range(block // HEAD):
                values_c[:, pl.ds(pl.multiple_of(r * block + b * HEAD, HEAD), HEAD)] = jnp.transpose(
                    turned[b * HEAD : (b + 1) * HEAD, :]
                ).astype(jnp.bfloat16)

        @pl.when(j > 0)
        def _():
            queries = []
            for h in range(2):
                value = product[:, h * HEAD : (h + 1) * HEAD] + qb_ref[j - 1, :, h * HEAD : (h + 1) * HEAD]
                queries.append(rotated(value, cosine, sine).astype(jnp.bfloat16))

            def write(h, value):
                results[j - 1, where, h * HEAD : (h + 1) * HEAD] = value

            attend_heads(r, queries, write)
            result_copy(r, j - 1).start()

        return 0

    lax.fori_loop(0, len(plan), unit, 0)

    for r in range(chunks):
        for j in range(columns):
            result_copy(r, j).wait()
    for n in range(3):
        for kind in range(2):
            prompt_copy(n, kind, joined).wait_send()
    for t in range(tps - 1):
        stat_copy(t).wait_send()
    for i in range(pieces):
        direct(i).wait_send()
        relay(i).wait_send()
    for r in range(chunks):
        to_sibling(tp, r).wait_send()
        pl.when(z < floors - 1)(lambda: own(r, 0).wait_send())
        pl.when(z > 0)(lambda: own(r, 1).wait_send())
        for f in range(floors):
            s = 2 * f + core

            @pl.when(z != f)
            def _():
                to_sibling(s, r).wait_send()

            @pl.when((f < z) & (z < floors - 1))
            def _():
                forward(s, r, up).wait_send()

            @pl.when((f > z) & (z > 0))
            def _():
                forward(s, r, down).wait_send()


def fits(prompt_inputs, cand_inputs, w_query, w_key):
    rows, part = cand_inputs.shape
    tps = lax.axis_size("tp")
    return (
        lax.axis_size("cache") == 2
        and lax.axis_size("cand") == 2
        and tps % 2 == 0
        and tps >= 4
        and rows == 4 * CLEN
        and w_key.shape[1] == HEAD
        and w_query.shape[1] == 8 * HEAD
        and part * tps == D
        and prompt_inputs.shape[0] % HEAD == 0
        and prompt_inputs.shape[0] <= 4 * HEAD
        and w_query.shape[0] == 4 * part
    )


def whole_layer(
    prompt_inputs,
    cand_inputs,
    norm_gain,
    w_query,
    w_key,
    w_value,
    q_bias,
    k_bias,
    v_bias,
    cand_lengths,
    prefix_ends,
):
    rows, part = cand_inputs.shape
    tps = lax.axis_size("tp")
    floors, chunks, wide = tps // 2, rows // CLEN, 2 * HEAD
    columns = w_query.shape[1] // wide
    pieces = 2 + 2 * columns
    prompt_rows = prompt_inputs.shape[0]
    half_freq = ROPE_THETA ** (-np.arange(HEAD // 2, dtype=np.float64) * 2.0 / HEAD)
    freq = jnp.asarray(np.concatenate([half_freq, half_freq]).astype(np.float32).reshape(1, HEAD))
    anywhere = pl.BlockSpec(memory_space=pl.ANY)
    vmem = pl.BlockSpec(memory_space=pltpu.VMEM)
    smem = pl.BlockSpec(memory_space=pltpu.SMEM)
    dma = pltpu.SemaphoreType.DMA
    return pl.pallas_call(
        layer_kernel,
        out_shape=jax.ShapeDtypeStruct((rows, columns * wide), jnp.bfloat16),
        in_specs=[anywhere, anywhere, vmem, anywhere, anywhere, anywhere, vmem, vmem, vmem, vmem, smem, smem],
        out_specs=anywhere,
        scratch_shapes=[
            pltpu.VMEM((tps, rows, part), jnp.bfloat16),
            pltpu.VMEM((1 + columns, part * tps, wide), jnp.bfloat16),
            pltpu.VMEM((prompt_rows, part * tps), jnp.bfloat16),
            pltpu.VMEM((rows, HEAD), jnp.float32),
            pltpu.VMEM((rows, HEAD), jnp.float32),
            pltpu.VMEM((tps, 1, rows), jnp.float32),
            pltpu.VMEM((4, prompt_rows, HEAD), jnp.bfloat16),
            pltpu.VMEM((4, HEAD, prompt_rows), jnp.bfloat16),
            pltpu.VMEM((rows, HEAD), jnp.bfloat16),
            pltpu.VMEM((HEAD, rows), jnp.bfloat16),
            pltpu.VMEM((chunks, 4, prompt_rows, HEAD), jnp.bfloat16),
            pltpu.VMEM((2, 4 * prompt_rows + CLEN, CLEN), jnp.float32),
            pltpu.VMEM((columns, rows, wide), jnp.bfloat16),
            dma((4 + columns,)),
            dma((pieces,)),
            dma((pieces,)),
            dma((pieces,)),
            dma((pieces,)),
            dma((2, chunks)),
            dma((tps, chunks)),
            dma((tps, chunks)),
            dma((tps, chunks)),
            dma((tps - 1,)),
            dma((tps,)),
            dma((3, 2)),
            dma((3, 2)),
            dma((chunks, columns)),
        ],
        compiler_params=pltpu.CompilerParams(
            collective_id=0, has_side_effects=True, vmem_limit_bytes=64 * 1024 * 1024 - 65536
        ),
        name="whole_layer",
    )(
        cand_inputs.reshape(rows, part),
        prompt_inputs,
        norm_gain.reshape(tps, 1, part),
        w_query,
        w_key,
        w_value,
        q_bias.reshape(columns, 1, wide),
        k_bias.reshape(1, HEAD),
        v_bias.reshape(1, HEAD),
        freq,
        prefix_ends,
        cand_lengths,
    )


def query_product(normed, w_query):
    caches = lax.axis_size("cache")
    cands = lax.axis_size("cand")
    depth = w_query.shape[0]
    if caches != 2 or cands != 2 or depth % 4 != 0:
        return jnp.dot(
            normed,
            lax.all_gather(w_query, "cache", axis=0, tiled=True),
            preferred_element_type=jnp.float32,
        )
    mine = lax.axis_index("cache")
    side = lax.axis_index("cand")
    part = depth // 4
    swap = [(0, 1), (1, 0)]
    direct = [
        lax.ppermute(
            lax.dynamic_slice_in_dim(w_query, (2 * side + turn) * part, part), "cache", swap
        )
        for turn in range(2)
    ]
    relayed = [lax.ppermute(piece, "cand", swap) for piece in direct]

    def product(first, weights):
        columns = lax.dynamic_slice_in_dim(normed, first, weights.shape[0], 1)
        return jnp.dot(columns, weights, preferred_element_type=jnp.float32)

    total = product(mine * depth, w_query)
    other = (1 - mine) * depth
    for turn in range(2):
        total = total + product(other + (2 * side + turn) * part, direct[turn])
    for turn in range(2):
        total = total + product(other + (2 * (1 - side) + turn) * part, relayed[turn])
    return total


def per_device(
    prompt_inputs,
    cand_inputs,
    norm_gain,
    w_query,
    w_key,
    w_value,
    q_bias,
    k_bias,
    v_bias,
    cand_lengths,
    prefix_ends,
):
    prompt_dev = prompt_inputs.shape[0]
    cand_dev = cand_inputs.shape[0]
    head_size = HEAD
    kv_local = w_key.shape[1] // head_size
    groups = HEADS // KV_HEADS
    kv_width = kv_local * head_size
    joined = lax.axis_index("cache") * lax.axis_size("cand") + lax.axis_index("cand")
    if fits(prompt_inputs, cand_inputs, w_query, w_key):
        return whole_layer(
            prompt_inputs,
            cand_inputs,
            norm_gain,
            w_query,
            w_key,
            w_value,
            q_bias,
            k_bias,
            v_bias,
            cand_lengths,
            prefix_ends,
        )
    widened_p = prompt_inputs.astype(jnp.float32)
    normed_p = (
        widened_p
        * lax.rsqrt(jnp.mean(widened_p * widened_p, axis=-1, keepdims=True) + EPSILON)
        * norm_gain
    ).astype(jnp.bfloat16)
    widened_c = cand_inputs.astype(jnp.float32)
    squares = lax.psum(jnp.sum(widened_c * widened_c, axis=-1), "tp")
    part_width = cand_inputs.shape[1]
    gain_part = lax.dynamic_slice_in_dim(norm_gain, lax.axis_index("tp") * part_width, part_width)
    normed_part = (widened_c * lax.rsqrt(squares / D + EPSILON)[:, None] * gain_part).astype(
        jnp.bfloat16
    )
    normed_c = lax.all_gather(normed_part, "tp", axis=1, tiled=True)
    row_ids = joined * cand_dev + jnp.arange(cand_dev, dtype=jnp.int32)
    prefix_row = row_lookup(row_ids, prefix_ends)
    cand_pos = prefix_row + row_ids % CLEN
    prompt_pos = joined * prompt_dev + jnp.arange(prompt_dev, dtype=jnp.int32)
    key_value = jnp.concatenate([w_key, w_value], axis=1)
    if lax.axis_size("cache") == 2:
        other_half = lax.ppermute(key_value, "cache", [(0, 1), (1, 0)])
        key_value = jnp.where(
            lax.axis_index("cache") == 0,
            jnp.concatenate([key_value, other_half], axis=0),
            jnp.concatenate([other_half, key_value], axis=0),
        )
    else:
        key_value = lax.all_gather(key_value, "cache", axis=0, tiled=True)
    kv_prompt = jnp.dot(normed_p, key_value, preferred_element_type=jnp.float32)

    def keys_values(product, positions):
        rows = product.shape[0]
        keys = rotate(
            (product[:, :kv_width] + k_bias).reshape(rows, kv_local, head_size), positions
        ).astype(jnp.bfloat16)
        values = (product[:, kv_width:] + v_bias).astype(jnp.bfloat16)
        values = values.reshape(rows, kv_local, head_size)
        return jnp.concatenate([keys, values], axis=2).reshape(rows, 2 * kv_width)

    kv_p = lax.all_gather(
        keys_values(kv_prompt, prompt_pos), ("cache", "cand"), axis=0, tiled=True
    )
    q_cand = query_product(normed_c, w_query)
    kv_c = keys_values(jnp.dot(normed_c, key_value, preferred_element_type=jnp.float32), cand_pos)
    queries = rotate(
        (q_cand + q_bias).reshape(cand_dev, kv_local * groups, head_size), cand_pos
    ).astype(jnp.bfloat16)
    tile_rows = min(cand_dev, CLEN)
    tile_first = joined * cand_dev + tile_rows * jnp.arange(cand_dev // tile_rows, dtype=jnp.int32)
    prefixes = row_lookup(tile_first, prefix_ends)
    lengths = row_lookup(tile_first, cand_lengths)
    offsets = tile_first % CLEN
    if cand_dev < CLEN:
        kv_c = lax.all_gather(kv_c, ("cache", "cand"), axis=0, tiled=True)
        kv_c = lax.dynamic_slice_in_dim(kv_c, joined * cand_dev // CLEN * CLEN, CLEN)
    return attend(
        prefixes,
        lengths,
        offsets,
        queries.reshape(cand_dev, kv_local * groups * head_size),
        kv_p,
        kv_c,
        kv_local,
        groups,
    )


def solution(mesh):
    placed = (
        P(("cache", "cand"), None),
        P(("cache", "cand"), "tp"),
        P(),
        P("cache", "tp"),
        P("cache", "tp"),
        P("cache", "tp"),
        P("tp"),
        P("tp"),
        P("tp"),
        P(),
        P(),
    )
    return jax.shard_map(
        per_device,
        mesh=mesh,
        in_specs=placed,
        out_specs=P(("cache", "cand"), "tp"),
        check_vma=False,
    )
```

```python
import functools
import math

import jax
import jax.numpy as jnp
import numpy as np
from jax import lax
from jax.experimental import pallas as pl
from jax.experimental.pallas import tpu as pltpu
from jax.sharding import PartitionSpec as P

D = 8192
HEADS = 64
KV_HEADS = 8
HEAD = 128
CANDS = 16
CLEN = 256


ROPE_THETA = 1000000.0
EPSILON = 1e-06


def rotate(tensor, positions):
    half_size = tensor.shape[-1] // 2
    inverse_freq = jnp.power(
        ROPE_THETA, -jnp.arange(half_size, dtype=jnp.float32) * 2.0 / tensor.shape[-1]
    )
    angles = positions.astype(jnp.float32)[:, None] * inverse_freq[None, :]
    cosine = jnp.cos(angles)[:, None, :]
    sine_part = jnp.sin(angles)[:, None, :]
    first_half = tensor[..., :half_size]
    second = tensor[..., half_size:]
    return jnp.concatenate(
        [first_half * cosine - second * sine_part, second * cosine + first_half * sine_part],
        axis=-1,
    )


def row_lookup(row_ids, table):
    chosen = (row_ids // CLEN)[:, None] == jnp.arange(CANDS, dtype=jnp.int32)[None, :]
    return jnp.sum(jnp.where(chosen, table[None, :], 0), axis=1)


def attend_kernel(
    prefix_ref, length_ref, offset_ref, q_ref, kvp_ref, kvc_ref, out_ref, *, heads, chunk, scale
):
    cand = pl.program_id(0)
    prefix = prefix_ref[cand]
    length = length_ref[cand]
    offset = offset_ref[cand]
    rows = q_ref.shape[0]
    contract = (((1,), (1,)), ((), ()))

    def scores_of(head, key_rows):
        return (
            lax.dot_general(
                q_ref[:, head * HEAD : (head + 1) * HEAD],
                key_rows,
                contract,
                preferred_element_type=jnp.float32,
            )
            * scale
        )

    def weighted(probabilities, value_rows):
        return jnp.dot(
            probabilities.astype(jnp.bfloat16), value_rows, preferred_element_type=jnp.float32
        )

    own_shape = (rows, kvc_ref.shape[0])
    causal = lax.broadcasted_iota(jnp.int32, own_shape, 1) <= offset + lax.broadcasted_iota(
        jnp.int32, own_shape, 0
    )
    state = []
    for head in range(heads):
        scores = jnp.where(causal, scores_of(head, kvc_ref[:, :HEAD]), -1e30)
        maxima = jnp.max(scores, axis=1, keepdims=True)
        probabilities = jnp.exp2(scores - maxima)
        totals = jnp.sum(probabilities, axis=1, keepdims=True)
        state += [maxima, totals, weighted(probabilities, kvc_ref[:, HEAD:])]

    def advance(turn, running):
        first = pl.multiple_of(turn * chunk, chunk)
        key_rows = kvp_ref[pl.ds(first, chunk), :HEAD]
        value_rows = kvp_ref[pl.ds(first, chunk), HEAD:]
        seen = first + lax.broadcasted_iota(jnp.int32, (rows, chunk), 1) < prefix
        following = []
        for head in range(heads):
            maxima, totals, accumulated = running[3 * head : 3 * head + 3]
            scores = jnp.where(seen, scores_of(head, key_rows), -1e30)
            new_maxima = jnp.maximum(maxima, jnp.max(scores, axis=1, keepdims=True))
            probabilities = jnp.exp2(scores - new_maxima)
            rescale = jnp.exp2(maxima - new_maxima)
            totals = totals * rescale + jnp.sum(probabilities, axis=1, keepdims=True)
            accumulated = accumulated * rescale + weighted(probabilities, value_rows)
            following += [new_maxima, totals, accumulated]
        return tuple(following)

    state = lax.fori_loop(0, (prefix + chunk - 1) // chunk, advance, tuple(state))
    valid = offset + lax.broadcasted_iota(jnp.int32, (rows, HEAD), 0) < length
    for head in range(heads):
        result = state[3 * head + 2] / state[3 * head + 1]
        out_ref[:, head * HEAD : (head + 1) * HEAD] = jnp.where(valid, result, 0.0).astype(
            jnp.bfloat16
        )


def attend(prefixes, lengths, offsets, queries, kv_prompt, kv_cand, kv_local, groups):
    tiles = prefixes.shape[0]
    rows = queries.shape[0] // tiles
    prompt = kv_prompt.shape[0]
    chunk = next(size for size in (512, 256, 128, prompt) if prompt % size == 0)
    heads = 2 if groups % 2 == 0 else 1
    turns = groups // heads
    return pl.pallas_call(
        functools.partial(
            attend_kernel, heads=heads, chunk=chunk, scale=HEAD ** (-0.5) * math.log2(math.e)
        ),
        grid_spec=pltpu.PrefetchScalarGridSpec(
            num_scalar_prefetch=3,
            grid=(tiles, kv_local, turns),
            in_specs=[
                pl.BlockSpec((rows, heads * HEAD), lambda c, k, t, *_: (c, k * turns + t)),
                pl.BlockSpec((prompt, 2 * HEAD), lambda c, k, t, *_: (0, k)),
                pl.BlockSpec((CLEN, 2 * HEAD), lambda c, k, t, *_: (c, k)),
            ],
            out_specs=pl.BlockSpec((rows, heads * HEAD), lambda c, k, t, *_: (c, k * turns + t)),
        ),
        out_shape=jax.ShapeDtypeStruct(queries.shape, jnp.bfloat16),
        cost_estimate=pl.CostEstimate(
            flops=4 * queries.size * (prompt + CLEN),
            bytes_accessed=4 * queries.size,
            transcendentals=queries.size // HEAD * (prompt + CLEN),
        ),
        compiler_params=pltpu.CompilerParams(vmem_limit_bytes=60 * 1024 * 1024),
    )(prefixes, lengths, offsets, queries, kv_prompt, kv_cand)


MESH = pl.DeviceIdType.MESH


def chunk_bounds(rows):
    whole = [(first, CLEN) for first in range(0, rows - CLEN, CLEN)]
    return whole + [(rows - CLEN, CLEN // 2), (rows - CLEN // 2, CLEN // 2)]


def piece_table(columns, quarter):
    table = [(0, 0, quarter), (0, 0, quarter)]
    for j in range(columns):
        count = 2 if j < columns - 1 else 4
        table += [(1 + j, n * (quarter // count), quarter // count) for n in range(count)]
    return table


def link_orders(depths, chunks):
    orders = [[(0, r) for r in range(chunks)]]
    for depth in range(1, depths):
        ready = {(d + 1, r): k + 2 for k, (d, r) in enumerate(orders[-1])}
        ready.update({(0, r): 0 for r in range(chunks)})
        order = []
        while ready:
            slot = len(order)
            able = [e for e in ready if ready[e] <= slot] or list(ready)
            pick = min(able, key=lambda e: (e[1], e[0]))
            del ready[pick]
            order.append(pick)
        orders.append(order)
    return orders


def layer_kernel(
    xc_ref, xp_ref, gain_ref, wq_ref, wk_ref, wv_ref, qb_ref, kb_ref, vb_ref, freq_ref, prefix_ref, length_ref,
    out_ref,
    acts, wts, prompt, cosines, sines, stats, keys_p, values_p, keys_c, values_c, hidden, scores, results,
    load_sem, wsend, wrecv, rsend, rrecv, own_sem, fwd_sem, sib_sem, arr_sem, st_send, st_recv, kp_send, kp_recv, out_sem,
):
    y, tp, x = lax.axis_index("cache"), lax.axis_index("tp"), lax.axis_index("cand")
    tps = lax.axis_size("tp")
    floors = tps // 2
    z, core = tp // 2, tp % 2
    rows, part = xc_ref.shape
    block = CLEN
    cands = rows // block
    bounds = chunk_bounds(rows)
    chunks = len(bounds)
    half = wq_ref.shape[0]
    quarter = half // 2
    wide = 2 * HEAD
    columns = wq_ref.shape[1] // wide
    table_of_pieces = piece_table(columns, quarter)
    pieces = len(table_of_pieces)
    prompt_rows = xp_ref.shape[0]
    slices = tps
    joined = y * 2 + x

    up, down, sib = (y, tp + 2, x), (y, tp - 2, x), (y, tp + 1 - 2 * core, x)
    over, aside, across = (1 - y, tp, x), (y, tp, 1 - x), (1 - y, tp, 1 - x)
    peers = [(y, (tp + t) % tps, x) for t in range(1, tps)]

    barrier = pltpu.get_barrier_semaphore()
    for peer in peers + [over, aside, across]:
        pl.semaphore_signal(barrier, inc=1, device_id=peer, device_id_type=MESH)

    load_x = pltpu.make_async_copy(xc_ref, acts.at[tp], load_sem.at[0])
    load_p = pltpu.make_async_copy(xp_ref, prompt, load_sem.at[1])
    own_rows = pl.ds(pl.multiple_of(y * half, half), half)
    load_w = [
        pltpu.make_async_copy(wk_ref, wts.at[0, own_rows, :HEAD], load_sem.at[2]),
        pltpu.make_async_copy(wv_ref, wts.at[0, own_rows, HEAD:], load_sem.at[3]),
    ] + [
        pltpu.make_async_copy(
            wq_ref.at[:, j * wide : (j + 1) * wide], wts.at[1 + j, own_rows, :], load_sem.at[4 + j]
        )
        for j in range(columns)
    ]
    load_x.start()
    load_p.start()
    for copy in load_w:
        copy.start()

    def piece_place(i, side_y, side_x):
        j, first, count = table_of_pieces[i]
        where = pl.ds(pl.multiple_of(side_y * half + side_x * quarter + first, count), count)
        return wts.at[0, where, i * HEAD : (i + 1) * HEAD] if j == 0 else wts.at[j, where, :]

    def direct(i):
        j, first, count = table_of_pieces[i]
        where = pl.ds(pl.multiple_of(x * quarter + first, count), count)
        src = (wk_ref, wv_ref)[i].at[where, :] if j == 0 else wq_ref.at[where, (j - 1) * wide : j * wide]
        return pltpu.make_async_remote_copy(
            src_ref=src, dst_ref=piece_place(i, y, x), send_sem=wsend.at[i], recv_sem=wrecv.at[i],
            device_id=over, device_id_type=MESH,
        )

    def relay(i):
        place = piece_place(i, 1 - y, x)
        return pltpu.make_async_remote_copy(
            src_ref=place, dst_ref=place, send_sem=rsend.at[i], recv_sem=rrecv.at[i],
            device_id=aside, device_id_type=MESH,
        )

    def pass_piece(i):
        if 0 <= i < pieces:
            direct(i).wait_recv()
            relay(i).start()

    def send_piece(i):
        if 0 <= i < pieces:
            direct(i).start()

    def slab(s, r):
        return acts.at[s, pl.ds(*bounds[r]), :]

    def slab_copy(s, r, send, target):
        return pltpu.make_async_remote_copy(
            src_ref=slab(s, r), dst_ref=slab(s, r), send_sem=send, recv_sem=arr_sem.at[s, r],
            device_id=target, device_id_type=MESH,
        )

    def to_sibling(s, r):
        return slab_copy(s, r, sib_sem.at[s, r], sib)

    def forward(s, r, target):
        return slab_copy(s, r, fwd_sem.at[s, r], target)

    def own(r, way):
        return slab_copy(tp, r, own_sem.at[way, r], (up, down)[way])

    orders = link_orders(floors - 1, chunks)
    longest = orders[-1]

    def link_event(k):
        if 0 <= k - 2 < len(longest):
            distance, r = longest[k - 2]

            @pl.when(z == 0)
            def _():
                s = tp + 2 * (distance + 1)
                forward(s, r, down).wait_recv()
                to_sibling(s, r).start()

            @pl.when(z == floors - 1)
            def _():
                s = tp - 2 * (distance + 1)
                forward(s, r, up).wait_recv()
                to_sibling(s, r).start()

        for depth, order in enumerate(orders):
            if k >= len(order):
                continue
            distance, r = order[k]

            def go(way, sign, target):
                if distance == 0:
                    own(r, way).start()
                else:
                    s = tp + sign * 2 * distance
                    copy = forward(s, r, target)
                    copy.wait_recv()
                    copy.start()
                    to_sibling(s, r).start()

            pl.when(z == depth)(functools.partial(go, 0, -1, up))
            pl.when(floors - 1 - z == depth)(functools.partial(go, 1, 1, down))

    load_x.wait()
    for r in range(cands):
        wide_x = acts[tp, pl.ds(r * block, block), :].astype(jnp.float32)
        squares = wide_x * wide_x
        lanes = squares[:, :HEAD]
        for t in range(1, part // HEAD):
            lanes = lanes + squares[:, t * HEAD : (t + 1) * HEAD]
        for b in range(block // HEAD):
            turned = jnp.transpose(lanes[b * HEAD : (b + 1) * HEAD, :])
            stats[tp, :, pl.ds(r * block + b * HEAD, HEAD)] = jnp.sum(turned, axis=0, keepdims=True)

    pl.semaphore_wait(barrier, tps + 2)

    def stat_copy(t):
        return pltpu.make_async_remote_copy(
            src_ref=stats.at[tp], dst_ref=stats.at[tp], send_sem=st_send.at[t], recv_sem=st_recv.at[tp],
            device_id=peers[t], device_id_type=MESH,
        )

    def stat_arrival(t):
        s = (tp + 1 + t) % tps
        return pltpu.make_async_remote_copy(
            src_ref=stats.at[s], dst_ref=stats.at[s], send_sem=st_send.at[t], recv_sem=st_recv.at[s],
            device_id=peers[t], device_id_type=MESH,
        )

    for t in range(tps - 1):
        stat_copy(t).start()
    for i in range(4):
        send_piece(i)
    for t in range(tps - 1):
        stat_arrival(t).wait_recv()
    total = stats[0]
    for s in range(1, tps):
        total = total + stats[s]
    inverse = lax.rsqrt(total / (part * tps) + EPSILON)

    for r in range(cands):
        line = jnp.broadcast_to(inverse[:, r * block : (r + 1) * block], (HEAD, block))
        column = jnp.concatenate(
            [jnp.transpose(line[:, b * HEAD : (b + 1) * HEAD]) for b in range(block // HEAD)], axis=0
        )
        column = jnp.concatenate([column] * (part // HEAD), axis=1)
        place = (tp, pl.ds(r * block, block), slice(None))
        acts[place] = (acts[place].astype(jnp.float32) * column * gain_ref[tp]).astype(jnp.bfloat16)
        if r == 1:
            link_event(0)
        if r >= 1:
            to_sibling(tp, r - 1).start()
    link_event(1)
    for r in range(cands - 1, chunks):
        to_sibling(tp, r).start()

    lane = lax.broadcasted_iota(jnp.int32, (1, HEAD), 1)
    sign = jnp.where(lane < HEAD // 2, -1.0, 1.0)

    def table(first, count):
        place = first + lax.broadcasted_iota(jnp.int32, (count, HEAD), 0)
        angles = place.astype(jnp.float32) * freq_ref[...]
        return jnp.cos(angles), jnp.sin(angles) * sign

    def fill(b, _):
        start = pl.multiple_of(b * HEAD, HEAD)
        cand = joined * cands + b // (block // HEAD)
        cosines[pl.ds(start, HEAD), :], sines[pl.ds(start, HEAD), :] = table(
            prefix_ref[cand] + b % (block // HEAD) * HEAD, HEAD
        )
        return 0

    lax.fori_loop(0, rows // HEAD, fill, 0)

    def hide(n, _):
        r, b = n // 4, n % 4
        key = b * prompt_rows + lax.broadcasted_iota(jnp.int32, (prompt_rows, HEAD), 0)
        first = lax.broadcasted_iota(jnp.int32, (prompt_rows, HEAD), 1) == 0
        unseen = first & (key >= prefix_ref[joined * cands + r])
        hidden[r, b] = jnp.where(unseen, -1e30, 0.0).astype(jnp.bfloat16)
        return 0

    lax.fori_loop(0, 4 * cands, hide, 0)
    later = pl.ds(*bounds[-1])
    keys_c[later, :] = jnp.zeros((bounds[-1][1], HEAD), jnp.bfloat16)
    values_c[:, later] = jnp.zeros((HEAD, bounds[-1][1]), jnp.bfloat16)

    def rotated(value, cosine, sine):
        return value * cosine + pltpu.roll(value, HEAD // 2, 1) * sine

    pass_piece(0)
    link_event(2)

    load_p.wait()
    slab_rows = 32

    def norm_prompt(b, _):
        where = pl.ds(pl.multiple_of(b * slab_rows, slab_rows), slab_rows)
        squares = jnp.zeros((slab_rows, 1), jnp.float32)
        for s in range(slices):
            value = prompt[where, s * part : (s + 1) * part].astype(jnp.float32)
            squares = squares + jnp.sum(value * value, axis=1, keepdims=True)
        scale = lax.rsqrt(squares / (part * slices) + EPSILON)
        for s in range(slices):
            value = prompt[where, s * part : (s + 1) * part].astype(jnp.float32)
            prompt[where, s * part : (s + 1) * part] = (value * scale * gain_ref[s]).astype(jnp.bfloat16)
        return 0

    lax.fori_loop(0, prompt_rows // slab_rows, norm_prompt, 0)
    pass_piece(1)
    link_event(3)
    pass_piece(2)
    link_event(4)

    def await_piece(i):
        place = piece_place(i, 1 - y, 1 - x)
        pltpu.make_async_remote_copy(
            src_ref=place, dst_ref=place, send_sem=rsend.at[i], recv_sem=rrecv.at[i],
            device_id=aside, device_id_type=MESH,
        ).wait_recv()

    load_w[0].wait()
    load_w[1].wait()
    for i in range(2):
        await_piece(i)

    def prompt_block(b, _):
        where = pl.ds(pl.multiple_of(b * HEAD, HEAD), HEAD)
        product = jnp.dot(prompt[where, :part], wts[0, :part, :], preferred_element_type=jnp.float32)
        for s in range(1, slices):
            product = product + jnp.dot(
                prompt[where, s * part : (s + 1) * part],
                wts[0, s * part : (s + 1) * part, :],
                preferred_element_type=jnp.float32,
            )
        cosine, sine = table(joined * prompt_rows + b * HEAD, HEAD)
        keys_p[joined, where, :] = rotated(product[:, :HEAD] + kb_ref[...], cosine, sine).astype(jnp.bfloat16)
        values_p[joined, :, where] = jnp.transpose(product[:, HEAD:] + vb_ref[...]).astype(jnp.bfloat16)
        return 0

    lax.fori_loop(0, prompt_rows // HEAD, prompt_block, 0)

    def prompt_copy(n, kind, slot):
        place = (keys_p, values_p)[kind].at[slot]
        return pltpu.make_async_remote_copy(
            src_ref=place, dst_ref=place, send_sem=kp_send.at[n, kind], recv_sem=kp_recv.at[n, kind],
            device_id=(over, aside, across)[n], device_id_type=MESH,
        )

    for n in range(3):
        for kind in range(2):
            prompt_copy(n, kind, joined).start()
    for i in range(4, 7):
        send_piece(i)
    pass_piece(3)
    link_event(5)
    for i in range(7, pieces):
        send_piece(i)

    def await_columns(j):
        load_w[2 + j].wait()
        for i in range(2, pieces):
            if table_of_pieces[i][0] == 1 + j:
                await_piece(i)

    def await_chunk(r):
        for f in range(floors):
            to_sibling(2 * f + 1 - core, r).wait_recv()

    def await_prompt(_):
        for n, slot in enumerate(((1 - y) * 2 + x, y * 2 + 1 - x, (1 - y) * 2 + 1 - x)):
            for kind in range(2):
                prompt_copy(n, kind, slot).wait_recv()

    def result_copy(n, j):
        where = pl.ds(*bounds[n]) if isinstance(n, int) else pl.ds(pl.multiple_of(n * block, block), block)
        return result_place(n, j, where)

    def result_place(n, j, where):
        across_columns = pl.ds(pl.multiple_of(j * wide, wide), wide)
        return pltpu.make_async_copy(
            results.at[j, where, :], out_ref.at[where, across_columns], out_sem.at[n, j]
        )

    factor = HEAD ** (-0.5) * math.log2(math.e)

    def attend_heads(r, own_rows, queries, valid, write):
        extra = jnp.where(lax.broadcasted_iota(jnp.int32, (block, HEAD), 1) == 0, 1.0, 0.0).astype(jnp.bfloat16)
        own_keys = pl.ds(pl.multiple_of(r * block, block), block)
        contract = (((1,), (1,)), ((), ()))
        states = [{} for _ in queries]

        def span(b):
            return slice(b * prompt_rows, (b + 1) * prompt_rows if b < 4 else 4 * prompt_rows + block)

        def score(h, b):
            state = states[h]
            if b < 4:
                found = lax.dot_general(
                    jnp.concatenate([keys_p[b], hidden[r, b]], axis=1),
                    jnp.concatenate([queries[h], extra], axis=1),
                    contract,
                    preferred_element_type=jnp.float32,
                )
            else:
                found = lax.dot_general(
                    keys_c[own_keys, :], queries[h], contract, preferred_element_type=jnp.float32
                )
                found = jnp.where(lax.broadcasted_iota(jnp.int32, (block, block), 0) <= own_rows, found, -1e30)
            scores[h, span(b), :] = found
            highest = jnp.max(found.reshape(-1, 8, block), axis=0)
            state["max"] = jnp.maximum(state["max"], highest) if "max" in state else highest
            if b == 4:
                state["max"] = jnp.max(state["max"], axis=0, keepdims=True) * factor

        def weigh(h, b):
            state = states[h]
            chances = jnp.exp2(scores[h, span(b), :] * factor - state["max"])
            total = jnp.sum(chances.reshape(-1, 8, block), axis=0)
            values = values_p[b] if b < 4 else values_c[:, own_keys]
            mixed = jnp.dot(values, chances.astype(jnp.bfloat16), preferred_element_type=jnp.float32)
            state["sum"] = state["sum"] + total if "sum" in state else total
            state["mix"] = state["mix"] + mixed if "mix" in state else mixed

        def finish(h):
            state = states[h]
            result = jnp.transpose(state["mix"] / jnp.sum(state["sum"], axis=0, keepdims=True))
            write(h, jnp.where(valid, result, 0.0).astype(jnp.bfloat16))

        count = len(queries)
        for b in range(5):
            score(0, b)
        for h in range(count):
            for b in range(5):
                weigh(h, b)
                if h + 1 < count:
                    score(h + 1, b)
            finish(h)

    def projected(where, j):
        product = jnp.dot(acts[0, where, :], wts[j, :part, :], preferred_element_type=jnp.float32)
        for s in range(1, slices):
            product = product + jnp.dot(
                acts[s, where, :], wts[j, s * part : (s + 1) * part, :], preferred_element_type=jnp.float32
            )
        return product

    def keep_keys(first, count, product, cosine, sine):
        keys_c[pl.ds(first, count), :] = rotated(product[:, :HEAD] + kb_ref[...], cosine, sine).astype(jnp.bfloat16)
        turned = product[:, HEAD:] + vb_ref[...]
        for b in range(count // HEAD):
            values_c[:, pl.ds(pl.multiple_of(first + b * HEAD, HEAD), HEAD)] = jnp.transpose(
                turned[b * HEAD : (b + 1) * HEAD, :]
            ).astype(jnp.bfloat16)

    def queries_of(j, product, cosine, sine):
        found = []
        for h in range(2):
            value = product[:, h * HEAD : (h + 1) * HEAD] + qb_ref[j - 1, :, h * HEAD : (h + 1) * HEAD]
            found.append(rotated(value, cosine, sine).astype(jnp.bfloat16))
        return found

    def whole_unit(r, j):
        first = pl.multiple_of(r * block, block)
        where = pl.ds(first, block)
        product = projected(where, j)
        cosine, sine = cosines[where, :], sines[where, :]
        pl.when(j == 0)(lambda: keep_keys(first, block, product, cosine, sine))

        @pl.when(j > 0)
        def _():
            queries = queries_of(j, product, cosine, sine)

            def write(h, value):
                results[j - 1, where, h * HEAD : (h + 1) * HEAD] = value

            valid = lax.broadcasted_iota(jnp.int32, (block, HEAD), 0) < length_ref[joined * cands + r]
            attend_heads(r, lax.broadcasted_iota(jnp.int32, (block, block), 1), queries, valid, write)
            result_copy(r, j - 1).start()

    def half_unit(n, j):
        count = block // 2
        r = cands - 1
        offset = (n - r) * count
        first = pl.multiple_of(r * block + offset, count)
        where = pl.ds(first, count)
        product = projected(where, j)
        cosine, sine = cosines[where, :], sines[where, :]
        pl.when(j == 0)(lambda: keep_keys(first, count, product, cosine, sine))

        @pl.when(j > 0)
        def _():
            queries = jnp.concatenate(queries_of(j, product, cosine, sine), axis=0)

            def write(_h, value):
                for h in range(2):
                    results[j - 1, where, h * HEAD : (h + 1) * HEAD] = value[h * count : (h + 1) * count, :]

            def own_row(axis, shape):
                place = lax.broadcasted_iota(jnp.int32, shape, axis)
                return offset + jnp.where(place < count, place, place - count)

            valid = own_row(0, (block, HEAD)) < length_ref[joined * cands + r]
            attend_heads(r, own_row(1, (block, block)), [queries], valid, write)
            result_place(n, j - 1, where).start()

    plan = []

    def add(events, *units):
        for n, unit in enumerate(units):
            plan.append((events if n == 0 else [], unit))

    E, P, C, J = link_event, pass_piece, await_chunk, await_columns
    add([(E, 6), (P, 4), (C, 0), (J, 0), (await_prompt, 0)], (0, 0), (0, 1))
    add([(E, 7), (C, 1)], (1, 0), (1, 1))
    add([(P, 5), (E, 8), (P, 6), (J, 1)], (0, 2), (1, 2))
    add([(E, 9), (P, 7), (P, 8), (E, 10), (C, 2)], (2, 0), (2, 1))
    add([(P, 9)], (2, 2))
    add([(E, 11), (J, 2)], (0, 3))
    add([(P, 10), (E, 12)], (1, 3), (2, 3))
    add([(P, 11), (E, 13), (C, 3)], (3, 0), (3, 1), (3, 2), (3, 3))
    add([(E, 14), (J, 3)], (0, 4), (1, 4))
    add([(E, 15)], (2, 4))
    add([(E, 16)], (3, 4))
    add([(C, 4)], (4, 0), (4, 1), (4, 2), (4, 3), (4, 4))

    def unit(u, _):
        for k, (events, _unit) in enumerate(plan):
            if events:

                @pl.when(u == k)
                def _():
                    for call, argument in events:
                        call(argument)

        r, j = 0, 0
        for k, (_events, (unit_r, unit_j)) in enumerate(plan):
            r = r + jnp.where(u == k, unit_r, 0)
            j = j + jnp.where(u == k, unit_j, 0)
        pl.when(r < cands - 1)(lambda: whole_unit(r, j))
        pl.when(r >= cands - 1)(lambda: half_unit(r, j))
        return 0

    lax.fori_loop(0, len(plan), unit, 0)

    for r in range(chunks):
        for j in range(columns):
            result_copy(r, j).wait()
    for n in range(3):
        for kind in range(2):
            prompt_copy(n, kind, joined).wait_send()
    for t in range(tps - 1):
        stat_copy(t).wait_send()
    for i in range(pieces):
        direct(i).wait_send()
        relay(i).wait_send()
    for r in range(chunks):
        to_sibling(tp, r).wait_send()
        pl.when(z < floors - 1)(lambda: own(r, 0).wait_send())
        pl.when(z > 0)(lambda: own(r, 1).wait_send())
        for f in range(floors):
            s = 2 * f + core

            @pl.when(z != f)
            def _():
                to_sibling(s, r).wait_send()

            @pl.when((f < z) & (z < floors - 1))
            def _():
                forward(s, r, up).wait_send()

            @pl.when((f > z) & (z > 0))
            def _():
                forward(s, r, down).wait_send()


def fits(prompt_inputs, cand_inputs, w_query, w_key):
    rows, part = cand_inputs.shape
    tps = lax.axis_size("tp")
    return (
        lax.axis_size("cache") == 2
        and lax.axis_size("cand") == 2
        and tps % 2 == 0
        and tps >= 4
        and rows == 4 * CLEN
        and w_key.shape[1] == HEAD
        and w_query.shape[1] == 8 * HEAD
        and part * tps == D
        and prompt_inputs.shape[0] % HEAD == 0
        and prompt_inputs.shape[0] <= 4 * HEAD
        and w_query.shape[0] == 4 * part
    )


def whole_layer(
    prompt_inputs,
    cand_inputs,
    norm_gain,
    w_query,
    w_key,
    w_value,
    q_bias,
    k_bias,
    v_bias,
    cand_lengths,
    prefix_ends,
):
    rows, part = cand_inputs.shape
    tps = lax.axis_size("tp")
    cands, wide = rows // CLEN, 2 * HEAD
    chunks = len(chunk_bounds(rows))
    columns = w_query.shape[1] // wide
    pieces = len(piece_table(columns, w_query.shape[0] // 2))
    prompt_rows = prompt_inputs.shape[0]
    half_freq = ROPE_THETA ** (-np.arange(HEAD // 2, dtype=np.float64) * 2.0 / HEAD)
    freq = jnp.asarray(np.concatenate([half_freq, half_freq]).astype(np.float32).reshape(1, HEAD))
    anywhere = pl.BlockSpec(memory_space=pl.ANY)
    vmem = pl.BlockSpec(memory_space=pltpu.VMEM)
    smem = pl.BlockSpec(memory_space=pltpu.SMEM)
    dma = pltpu.SemaphoreType.DMA
    return pl.pallas_call(
        layer_kernel,
        out_shape=jax.ShapeDtypeStruct((rows, columns * wide), jnp.bfloat16),
        in_specs=[anywhere, anywhere, vmem, anywhere, anywhere, anywhere, vmem, vmem, vmem, vmem, smem, smem],
        out_specs=anywhere,
        scratch_shapes=[
            pltpu.VMEM((tps, rows, part), jnp.bfloat16),
            pltpu.VMEM((1 + columns, part * tps, wide), jnp.bfloat16),
            pltpu.VMEM((prompt_rows, part * tps), jnp.bfloat16),
            pltpu.VMEM((rows, HEAD), jnp.float32),
            pltpu.VMEM((rows, HEAD), jnp.float32),
            pltpu.VMEM((tps, 1, rows), jnp.float32),
            pltpu.VMEM((4, prompt_rows, HEAD), jnp.bfloat16),
            pltpu.VMEM((4, HEAD, prompt_rows), jnp.bfloat16),
            pltpu.VMEM((rows, HEAD), jnp.bfloat16),
            pltpu.VMEM((HEAD, rows), jnp.bfloat16),
            pltpu.VMEM((cands, 4, prompt_rows, HEAD), jnp.bfloat16),
            pltpu.VMEM((2, 4 * prompt_rows + CLEN, CLEN), jnp.float32),
            pltpu.VMEM((columns, rows, wide), jnp.bfloat16),
            dma((4 + columns,)),
            dma((pieces,)),
            dma((pieces,)),
            dma((pieces,)),
            dma((pieces,)),
            dma((2, chunks)),
            dma((tps, chunks)),
            dma((tps, chunks)),
            dma((tps, chunks)),
            dma((tps - 1,)),
            dma((tps,)),
            dma((3, 2)),
            dma((3, 2)),
            dma((chunks, columns)),
        ],
        compiler_params=pltpu.CompilerParams(
            collective_id=0, has_side_effects=True, vmem_limit_bytes=64 * 1024 * 1024 - 65536
        ),
        name="whole_layer",
    )(
        cand_inputs.reshape(rows, part),
        prompt_inputs,
        norm_gain.reshape(tps, 1, part),
        w_query,
        w_key,
        w_value,
        q_bias.reshape(columns, 1, wide),
        k_bias.reshape(1, HEAD),
        v_bias.reshape(1, HEAD),
        freq,
        prefix_ends,
        cand_lengths,
    )


def query_product(normed, w_query):
    caches = lax.axis_size("cache")
    cands = lax.axis_size("cand")
    depth = w_query.shape[0]
    if caches != 2 or cands != 2 or depth % 4 != 0:
        return jnp.dot(
            normed,
            lax.all_gather(w_query, "cache", axis=0, tiled=True),
            preferred_element_type=jnp.float32,
        )
    mine = lax.axis_index("cache")
    side = lax.axis_index("cand")
    part = depth // 4
    swap = [(0, 1), (1, 0)]
    direct = [
        lax.ppermute(
            lax.dynamic_slice_in_dim(w_query, (2 * side + turn) * part, part), "cache", swap
        )
        for turn in range(2)
    ]
    relayed = [lax.ppermute(piece, "cand", swap) for piece in direct]

    def product(first, weights):
        columns = lax.dynamic_slice_in_dim(normed, first, weights.shape[0], 1)
        return jnp.dot(columns, weights, preferred_element_type=jnp.float32)

    total = product(mine * depth, w_query)
    other = (1 - mine) * depth
    for turn in range(2):
        total = total + product(other + (2 * side + turn) * part, direct[turn])
    for turn in range(2):
        total = total + product(other + (2 * (1 - side) + turn) * part, relayed[turn])
    return total


def per_device(
    prompt_inputs,
    cand_inputs,
    norm_gain,
    w_query,
    w_key,
    w_value,
    q_bias,
    k_bias,
    v_bias,
    cand_lengths,
    prefix_ends,
):
    prompt_dev = prompt_inputs.shape[0]
    cand_dev = cand_inputs.shape[0]
    head_size = HEAD
    kv_local = w_key.shape[1] // head_size
    groups = HEADS // KV_HEADS
    kv_width = kv_local * head_size
    joined = lax.axis_index("cache") * lax.axis_size("cand") + lax.axis_index("cand")
    if fits(prompt_inputs, cand_inputs, w_query, w_key):
        return whole_layer(
            prompt_inputs,
            cand_inputs,
            norm_gain,
            w_query,
            w_key,
            w_value,
            q_bias,
            k_bias,
            v_bias,
            cand_lengths,
            prefix_ends,
        )
    widened_p = prompt_inputs.astype(jnp.float32)
    normed_p = (
        widened_p
        * lax.rsqrt(jnp.mean(widened_p * widened_p, axis=-1, keepdims=True) + EPSILON)
        * norm_gain
    ).astype(jnp.bfloat16)
    widened_c = cand_inputs.astype(jnp.float32)
    squares = lax.psum(jnp.sum(widened_c * widened_c, axis=-1), "tp")
    part_width = cand_inputs.shape[1]
    gain_part = lax.dynamic_slice_in_dim(norm_gain, lax.axis_index("tp") * part_width, part_width)
    normed_part = (widened_c * lax.rsqrt(squares / D + EPSILON)[:, None] * gain_part).astype(
        jnp.bfloat16
    )
    normed_c = lax.all_gather(normed_part, "tp", axis=1, tiled=True)
    row_ids = joined * cand_dev + jnp.arange(cand_dev, dtype=jnp.int32)
    prefix_row = row_lookup(row_ids, prefix_ends)
    cand_pos = prefix_row + row_ids % CLEN
    prompt_pos = joined * prompt_dev + jnp.arange(prompt_dev, dtype=jnp.int32)
    key_value = jnp.concatenate([w_key, w_value], axis=1)
    if lax.axis_size("cache") == 2:
        other_half = lax.ppermute(key_value, "cache", [(0, 1), (1, 0)])
        key_value = jnp.where(
            lax.axis_index("cache") == 0,
            jnp.concatenate([key_value, other_half], axis=0),
            jnp.concatenate([other_half, key_value], axis=0),
        )
    else:
        key_value = lax.all_gather(key_value, "cache", axis=0, tiled=True)
    kv_prompt = jnp.dot(normed_p, key_value, preferred_element_type=jnp.float32)

    def keys_values(product, positions):
        rows = product.shape[0]
        keys = rotate(
            (product[:, :kv_width] + k_bias).reshape(rows, kv_local, head_size), positions
        ).astype(jnp.bfloat16)
        values = (product[:, kv_width:] + v_bias).astype(jnp.bfloat16)
        values = values.reshape(rows, kv_local, head_size)
        return jnp.concatenate([keys, values], axis=2).reshape(rows, 2 * kv_width)

    kv_p = lax.all_gather(
        keys_values(kv_prompt, prompt_pos), ("cache", "cand"), axis=0, tiled=True
    )
    q_cand = query_product(normed_c, w_query)
    kv_c = keys_values(jnp.dot(normed_c, key_value, preferred_element_type=jnp.float32), cand_pos)
    queries = rotate(
        (q_cand + q_bias).reshape(cand_dev, kv_local * groups, head_size), cand_pos
    ).astype(jnp.bfloat16)
    tile_rows = min(cand_dev, CLEN)
    tile_first = joined * cand_dev + tile_rows * jnp.arange(cand_dev // tile_rows, dtype=jnp.int32)
    prefixes = row_lookup(tile_first, prefix_ends)
    lengths = row_lookup(tile_first, cand_lengths)
    offsets = tile_first % CLEN
    if cand_dev < CLEN:
        kv_c = lax.all_gather(kv_c, ("cache", "cand"), axis=0, tiled=True)
        kv_c = lax.dynamic_slice_in_dim(kv_c, joined * cand_dev // CLEN * CLEN, CLEN)
    return attend(
        prefixes,
        lengths,
        offsets,
        queries.reshape(cand_dev, kv_local * groups * head_size),
        kv_p,
        kv_c,
        kv_local,
        groups,
    )


def solution(mesh):
    placed = (
        P(("cache", "cand"), None),
        P(("cache", "cand"), "tp"),
        P(),
        P("cache", "tp"),
        P("cache", "tp"),
        P("cache", "tp"),
        P("tp"),
        P("tp"),
        P("tp"),
        P(),
        P(),
    )
    return jax.shard_map(
        per_device,
        mesh=mesh,
        in_specs=placed,
        out_specs=P(("cache", "cand"), "tp"),
        check_vma=False,
    )
```

```python
import functools
import math

import jax
import jax.numpy as jnp
import numpy as np
from jax import lax
from jax.experimental import pallas as pl
from jax.experimental.pallas import tpu as pltpu
from jax.sharding import PartitionSpec as P

D = 8192
HEADS = 64
KV_HEADS = 8
HEAD = 128
CANDS = 16
CLEN = 256


ROPE_THETA = 1000000.0
EPSILON = 1e-06


def rotate(tensor, positions):
    half_size = tensor.shape[-1] // 2
    inverse_freq = jnp.power(
        ROPE_THETA, -jnp.arange(half_size, dtype=jnp.float32) * 2.0 / tensor.shape[-1]
    )
    angles = positions.astype(jnp.float32)[:, None] * inverse_freq[None, :]
    cosine = jnp.cos(angles)[:, None, :]
    sine_part = jnp.sin(angles)[:, None, :]
    first_half = tensor[..., :half_size]
    second = tensor[..., half_size:]
    return jnp.concatenate(
        [first_half * cosine - second * sine_part, second * cosine + first_half * sine_part],
        axis=-1,
    )


def row_lookup(row_ids, table):
    chosen = (row_ids // CLEN)[:, None] == jnp.arange(CANDS, dtype=jnp.int32)[None, :]
    return jnp.sum(jnp.where(chosen, table[None, :], 0), axis=1)


def attend_kernel(
    prefix_ref, length_ref, offset_ref, q_ref, kvp_ref, kvc_ref, out_ref, *, heads, chunk, scale
):
    cand = pl.program_id(0)
    prefix = prefix_ref[cand]
    length = length_ref[cand]
    offset = offset_ref[cand]
    rows = q_ref.shape[0]
    contract = (((1,), (1,)), ((), ()))

    def scores_of(head, key_rows):
        return (
            lax.dot_general(
                q_ref[:, head * HEAD : (head + 1) * HEAD],
                key_rows,
                contract,
                preferred_element_type=jnp.float32,
            )
            * scale
        )

    def weighted(probabilities, value_rows):
        return jnp.dot(
            probabilities.astype(jnp.bfloat16), value_rows, preferred_element_type=jnp.float32
        )

    own_shape = (rows, kvc_ref.shape[0])
    causal = lax.broadcasted_iota(jnp.int32, own_shape, 1) <= offset + lax.broadcasted_iota(
        jnp.int32, own_shape, 0
    )
    state = []
    for head in range(heads):
        scores = jnp.where(causal, scores_of(head, kvc_ref[:, :HEAD]), -1e30)
        maxima = jnp.max(scores, axis=1, keepdims=True)
        probabilities = jnp.exp2(scores - maxima)
        totals = jnp.sum(probabilities, axis=1, keepdims=True)
        state += [maxima, totals, weighted(probabilities, kvc_ref[:, HEAD:])]

    def advance(turn, running):
        first = pl.multiple_of(turn * chunk, chunk)
        key_rows = kvp_ref[pl.ds(first, chunk), :HEAD]
        value_rows = kvp_ref[pl.ds(first, chunk), HEAD:]
        seen = first + lax.broadcasted_iota(jnp.int32, (rows, chunk), 1) < prefix
        following = []
        for head in range(heads):
            maxima, totals, accumulated = running[3 * head : 3 * head + 3]
            scores = jnp.where(seen, scores_of(head, key_rows), -1e30)
            new_maxima = jnp.maximum(maxima, jnp.max(scores, axis=1, keepdims=True))
            probabilities = jnp.exp2(scores - new_maxima)
            rescale = jnp.exp2(maxima - new_maxima)
            totals = totals * rescale + jnp.sum(probabilities, axis=1, keepdims=True)
            accumulated = accumulated * rescale + weighted(probabilities, value_rows)
            following += [new_maxima, totals, accumulated]
        return tuple(following)

    state = lax.fori_loop(0, (prefix + chunk - 1) // chunk, advance, tuple(state))
    valid = offset + lax.broadcasted_iota(jnp.int32, (rows, HEAD), 0) < length
    for head in range(heads):
        result = state[3 * head + 2] / state[3 * head + 1]
        out_ref[:, head * HEAD : (head + 1) * HEAD] = jnp.where(valid, result, 0.0).astype(
            jnp.bfloat16
        )


def attend(prefixes, lengths, offsets, queries, kv_prompt, kv_cand, kv_local, groups):
    tiles = prefixes.shape[0]
    rows = queries.shape[0] // tiles
    prompt = kv_prompt.shape[0]
    chunk = next(size for size in (512, 256, 128, prompt) if prompt % size == 0)
    heads = 2 if groups % 2 == 0 else 1
    turns = groups // heads
    return pl.pallas_call(
        functools.partial(
            attend_kernel, heads=heads, chunk=chunk, scale=HEAD ** (-0.5) * math.log2(math.e)
        ),
        grid_spec=pltpu.PrefetchScalarGridSpec(
            num_scalar_prefetch=3,
            grid=(tiles, kv_local, turns),
            in_specs=[
                pl.BlockSpec((rows, heads * HEAD), lambda c, k, t, *_: (c, k * turns + t)),
                pl.BlockSpec((prompt, 2 * HEAD), lambda c, k, t, *_: (0, k)),
                pl.BlockSpec((CLEN, 2 * HEAD), lambda c, k, t, *_: (c, k)),
            ],
            out_specs=pl.BlockSpec((rows, heads * HEAD), lambda c, k, t, *_: (c, k * turns + t)),
        ),
        out_shape=jax.ShapeDtypeStruct(queries.shape, jnp.bfloat16),
        cost_estimate=pl.CostEstimate(
            flops=4 * queries.size * (prompt + CLEN),
            bytes_accessed=4 * queries.size,
            transcendentals=queries.size // HEAD * (prompt + CLEN),
        ),
        compiler_params=pltpu.CompilerParams(vmem_limit_bytes=60 * 1024 * 1024),
    )(prefixes, lengths, offsets, queries, kv_prompt, kv_cand)


MESH = pl.DeviceIdType.MESH


def chunk_bounds(rows):
    whole = [(first, CLEN) for first in range(0, rows - CLEN, CLEN)]
    return whole + [(rows - CLEN, CLEN // 2), (rows - CLEN // 2, CLEN // 2)]


def piece_table(columns, quarter):
    table = [(0, 0, 0, quarter // 2), (0, 0, quarter // 2, quarter // 2), (0, 1, 0, quarter)]
    for j in range(columns):
        count = 2 if j < columns - 1 else 4
        table += [(1 + j, None, n * (quarter // count), quarter // count) for n in range(count)]
    return table


def link_orders(depths, chunks):
    orders = [[(0, r) for r in range(chunks)]]
    for depth in range(1, depths):
        ready = {(d + 1, r): k + 2 for k, (d, r) in enumerate(orders[-1])}
        ready.update({(0, r): 0 for r in range(chunks)})
        order = []
        while ready:
            slot = len(order)
            able = [e for e in ready if ready[e] <= slot] or list(ready)
            pick = min(able, key=lambda e: (e[1], e[0]))
            del ready[pick]
            order.append(pick)
        orders.append(order)
    return orders


def layer_kernel(
    xc_ref, xp_ref, gain_ref, wq_ref, wk_ref, wv_ref, qb_ref, kb_ref, vb_ref, freq_ref, prefix_ref, length_ref,
    out_ref,
    acts, wts, prompt, cosines, sines, stats, keys_p, values_p, keys_c, values_c, hidden, scores, results,
    load_sem, wsend, wrecv, rsend, rrecv, own_sem, fwd_sem, sib_sem, arr_sem, st_send, st_recv, kp_send, kp_recv, out_sem,
):
    y, tp, x = lax.axis_index("cache"), lax.axis_index("tp"), lax.axis_index("cand")
    tps = lax.axis_size("tp")
    floors = tps // 2
    z, core = tp // 2, tp % 2
    rows, part = xc_ref.shape
    block = CLEN
    cands = rows // block
    bounds = chunk_bounds(rows)
    chunks = len(bounds)
    half = wq_ref.shape[0]
    quarter = half // 2
    wide = 2 * HEAD
    columns = wq_ref.shape[1] // wide
    table_of_pieces = piece_table(columns, quarter)
    pieces = len(table_of_pieces)
    prompt_rows = xp_ref.shape[0]
    slices = tps
    joined = y * 2 + x

    up, down, sib = (y, tp + 2, x), (y, tp - 2, x), (y, tp + 1 - 2 * core, x)
    over, aside, across = (1 - y, tp, x), (y, tp, 1 - x), (1 - y, tp, 1 - x)
    peers = [(y, (tp + t) % tps, x) for t in range(1, tps)]

    barrier = pltpu.get_barrier_semaphore()
    for peer in peers + [over, aside, across]:
        pl.semaphore_signal(barrier, inc=1, device_id=peer, device_id_type=MESH)

    load_x = pltpu.make_async_copy(xc_ref, acts.at[tp], load_sem.at[0])
    load_p = pltpu.make_async_copy(xp_ref, prompt, load_sem.at[1])
    own_rows = pl.ds(pl.multiple_of(y * half, half), half)
    load_w = [
        pltpu.make_async_copy(wk_ref, wts.at[0, own_rows, :HEAD], load_sem.at[2]),
        pltpu.make_async_copy(wv_ref, wts.at[0, own_rows, HEAD:], load_sem.at[3]),
    ] + [
        pltpu.make_async_copy(
            wq_ref.at[:, j * wide : (j + 1) * wide], wts.at[1 + j, own_rows, :], load_sem.at[4 + j]
        )
        for j in range(columns)
    ]
    load_x.start()
    load_p.start()
    for copy in load_w:
        copy.start()

    def piece_place(i, side_y, side_x):
        j, side, first, count = table_of_pieces[i]
        where = pl.ds(pl.multiple_of(side_y * half + side_x * quarter + first, count), count)
        return wts.at[0, where, side * HEAD : (side + 1) * HEAD] if j == 0 else wts.at[j, where, :]

    relayed = pieces - 1

    def direct(n):
        i, side_x = (n, x) if n < pieces else (pieces - 1, 1 - x)
        j, side, first, count = table_of_pieces[i]
        where = pl.ds(pl.multiple_of(side_x * quarter + first, count), count)
        src = (wk_ref, wv_ref)[side].at[where, :] if j == 0 else wq_ref.at[where, (j - 1) * wide : j * wide]
        return pltpu.make_async_remote_copy(
            src_ref=src, dst_ref=piece_place(i, y, side_x), send_sem=wsend.at[n], recv_sem=wrecv.at[n],
            device_id=over, device_id_type=MESH,
        )

    def relay(i):
        place = piece_place(i, 1 - y, x)
        return pltpu.make_async_remote_copy(
            src_ref=place, dst_ref=place, send_sem=rsend.at[i], recv_sem=rrecv.at[i],
            device_id=aside, device_id_type=MESH,
        )

    def pass_piece(i):
        direct(i).wait_recv()
        relay(i).start()

    def send_piece(i):
        direct(i).start()

    def slab(s, r):
        return acts.at[s, pl.ds(*bounds[r]), :]

    def slab_copy(s, r, send, target):
        return pltpu.make_async_remote_copy(
            src_ref=slab(s, r), dst_ref=slab(s, r), send_sem=send, recv_sem=arr_sem.at[s, r],
            device_id=target, device_id_type=MESH,
        )

    def to_sibling(s, r):
        return slab_copy(s, r, sib_sem.at[s, r], sib)

    def forward(s, r, target):
        return slab_copy(s, r, fwd_sem.at[s, r], target)

    def own(r, way):
        return slab_copy(tp, r, own_sem.at[way, r], (up, down)[way])

    orders = link_orders(floors - 1, chunks)
    longest = orders[-1]

    def link_event(k):
        if 0 <= k - 2 < len(longest):
            distance, r = longest[k - 2]

            @pl.when(z == 0)
            def _():
                s = tp + 2 * (distance + 1)
                forward(s, r, down).wait_recv()
                to_sibling(s, r).start()

            @pl.when(z == floors - 1)
            def _():
                s = tp - 2 * (distance + 1)
                forward(s, r, up).wait_recv()
                to_sibling(s, r).start()

        for depth, order in enumerate(orders):
            if k >= len(order):
                continue
            distance, r = order[k]

            def go(way, sign, target):
                if distance == 0:
                    own(r, way).start()
                else:
                    s = tp + sign * 2 * distance
                    copy = forward(s, r, target)
                    copy.wait_recv()
                    copy.start()
                    to_sibling(s, r).start()

            pl.when(z == depth)(functools.partial(go, 0, -1, up))
            pl.when(floors - 1 - z == depth)(functools.partial(go, 1, 1, down))

    pl.semaphore_wait(barrier, tps + 2)
    for i in range(5):
        send_piece(i)

    load_x.wait()
    for r in range(cands):
        wide_x = acts[tp, pl.ds(r * block, block), :].astype(jnp.float32)
        squares = wide_x * wide_x
        lanes = squares[:, :HEAD]
        for t in range(1, part // HEAD):
            lanes = lanes + squares[:, t * HEAD : (t + 1) * HEAD]
        for b in range(block // HEAD):
            turned = jnp.transpose(lanes[b * HEAD : (b + 1) * HEAD, :])
            stats[tp, :, pl.ds(r * block + b * HEAD, HEAD)] = jnp.sum(turned, axis=0, keepdims=True)

    def stat_copy(t):
        return pltpu.make_async_remote_copy(
            src_ref=stats.at[tp], dst_ref=stats.at[tp], send_sem=st_send.at[t], recv_sem=st_recv.at[tp],
            device_id=peers[t], device_id_type=MESH,
        )

    def stat_arrival(t):
        s = (tp + 1 + t) % tps
        return pltpu.make_async_remote_copy(
            src_ref=stats.at[s], dst_ref=stats.at[s], send_sem=st_send.at[t], recv_sem=st_recv.at[s],
            device_id=peers[t], device_id_type=MESH,
        )

    for t in range(tps - 1):
        stat_copy(t).start()
    for t in range(tps - 1):
        stat_arrival(t).wait_recv()
    total = stats[0]
    for s in range(1, tps):
        total = total + stats[s]
    inverse = lax.rsqrt(total / (part * tps) + EPSILON)

    for r in range(cands):
        line = jnp.broadcast_to(inverse[:, r * block : (r + 1) * block], (HEAD, block))
        column = jnp.concatenate(
            [jnp.transpose(line[:, b * HEAD : (b + 1) * HEAD]) for b in range(block // HEAD)], axis=0
        )
        column = jnp.concatenate([column] * (part // HEAD), axis=1)
        place = (tp, pl.ds(r * block, block), slice(None))
        acts[place] = (acts[place].astype(jnp.float32) * column * gain_ref[tp]).astype(jnp.bfloat16)
        if r == 1:
            link_event(0)
        if r >= 1:
            to_sibling(tp, r - 1).start()
    link_event(1)
    for r in range(cands - 1, chunks):
        to_sibling(tp, r).start()

    lane = lax.broadcasted_iota(jnp.int32, (1, HEAD), 1)
    sign = jnp.where(lane < HEAD // 2, -1.0, 1.0)

    def table(first, count):
        place = first + lax.broadcasted_iota(jnp.int32, (count, HEAD), 0)
        angles = place.astype(jnp.float32) * freq_ref[...]
        return jnp.cos(angles), jnp.sin(angles) * sign

    def fill(b, _):
        start = pl.multiple_of(b * HEAD, HEAD)
        cand = joined * cands + b // (block // HEAD)
        cosines[pl.ds(start, HEAD), :], sines[pl.ds(start, HEAD), :] = table(
            prefix_ref[cand] + b % (block // HEAD) * HEAD, HEAD
        )
        return 0

    lax.fori_loop(0, rows // HEAD, fill, 0)

    def hide(n, _):
        r, b = n // 4, n % 4
        key = b * prompt_rows + lax.broadcasted_iota(jnp.int32, (prompt_rows, HEAD), 0)
        first = lax.broadcasted_iota(jnp.int32, (prompt_rows, HEAD), 1) == 0
        unseen = first & (key >= prefix_ref[joined * cands + r])
        hidden[r, b] = jnp.where(unseen, -1e30, 0.0).astype(jnp.bfloat16)
        return 0

    lax.fori_loop(0, 4 * cands, hide, 0)
    later = pl.ds(*bounds[-1])
    keys_c[later, :] = jnp.zeros((bounds[-1][1], HEAD), jnp.bfloat16)
    values_c[:, later] = jnp.zeros((HEAD, bounds[-1][1]), jnp.bfloat16)

    def rotated(value, cosine, sine):
        return value * cosine + pltpu.roll(value, HEAD // 2, 1) * sine

    pass_piece(0)
    pass_piece(1)
    link_event(2)

    load_p.wait()
    slab_rows = 32

    def norm_prompt(b, _):
        where = pl.ds(pl.multiple_of(b * slab_rows, slab_rows), slab_rows)
        squares = jnp.zeros((slab_rows, 1), jnp.float32)
        for s in range(slices):
            value = prompt[where, s * part : (s + 1) * part].astype(jnp.float32)
            squares = squares + jnp.sum(value * value, axis=1, keepdims=True)
        scale = lax.rsqrt(squares / (part * slices) + EPSILON)
        for s in range(slices):
            value = prompt[where, s * part : (s + 1) * part].astype(jnp.float32)
            prompt[where, s * part : (s + 1) * part] = (value * scale * gain_ref[s]).astype(jnp.bfloat16)
        return 0

    lax.fori_loop(0, prompt_rows // slab_rows, norm_prompt, 0)
    pass_piece(2)
    link_event(3)
    pass_piece(3)
    link_event(4)

    def await_piece(i):
        place = piece_place(i, 1 - y, 1 - x)
        pltpu.make_async_remote_copy(
            src_ref=place, dst_ref=place, send_sem=rsend.at[i], recv_sem=rrecv.at[i],
            device_id=aside, device_id_type=MESH,
        ).wait_recv()

    load_w[0].wait()
    load_w[1].wait()
    for i in range(3):
        await_piece(i)

    def prompt_block(b, _):
        where = pl.ds(pl.multiple_of(b * HEAD, HEAD), HEAD)
        product = jnp.dot(prompt[where, :part], wts[0, :part, :], preferred_element_type=jnp.float32)
        for s in range(1, slices):
            product = product + jnp.dot(
                prompt[where, s * part : (s + 1) * part],
                wts[0, s * part : (s + 1) * part, :],
                preferred_element_type=jnp.float32,
            )
        cosine, sine = table(joined * prompt_rows + b * HEAD, HEAD)
        keys_p[joined, where, :] = rotated(product[:, :HEAD] + kb_ref[...], cosine, sine).astype(jnp.bfloat16)
        values_p[joined, :, where] = jnp.transpose(product[:, HEAD:] + vb_ref[...]).astype(jnp.bfloat16)
        return 0

    lax.fori_loop(0, prompt_rows // HEAD, prompt_block, 0)

    def prompt_copy(n, kind, slot):
        place = (keys_p, values_p)[kind].at[slot]
        return pltpu.make_async_remote_copy(
            src_ref=place, dst_ref=place, send_sem=kp_send.at[n, kind], recv_sem=kp_recv.at[n, kind],
            device_id=(over, aside, across)[n], device_id_type=MESH,
        )

    for n in range(3):
        for kind in range(2):
            prompt_copy(n, kind, joined).start()
    for i in range(5, 8):
        send_piece(i)
    pass_piece(4)
    link_event(5)
    for i in range(8, pieces + 1):
        send_piece(i)

    def await_columns(j):
        load_w[2 + j].wait()
        for i in range(pieces):
            if table_of_pieces[i][0] == 1 + j and i < relayed:
                await_piece(i)
        if j == columns - 1:
            direct(pieces - 1).wait_recv()
            direct(pieces).wait_recv()

    def await_chunk(r):
        for f in range(floors):
            to_sibling(2 * f + 1 - core, r).wait_recv()

    def await_prompt(_):
        for n, slot in enumerate(((1 - y) * 2 + x, y * 2 + 1 - x, (1 - y) * 2 + 1 - x)):
            for kind in range(2):
                prompt_copy(n, kind, slot).wait_recv()

    def result_copy(n, j):
        where = pl.ds(*bounds[n]) if isinstance(n, int) else pl.ds(pl.multiple_of(n * block, block), block)
        return result_place(n, j, where)

    def result_place(n, j, where):
        across_columns = pl.ds(pl.multiple_of(j * wide, wide), wide)
        return pltpu.make_async_copy(
            results.at[j, where, :], out_ref.at[where, across_columns], out_sem.at[n, j]
        )

    factor = HEAD ** (-0.5) * math.log2(math.e)

    def attend_heads(r, own_rows, queries, valid, write):
        extra = jnp.where(lax.broadcasted_iota(jnp.int32, (block, HEAD), 1) == 0, 1.0, 0.0).astype(jnp.bfloat16)
        own_keys = pl.ds(pl.multiple_of(r * block, block), block)
        contract = (((1,), (1,)), ((), ()))
        states = [{} for _ in queries]

        def span(b):
            return slice(b * prompt_rows, (b + 1) * prompt_rows if b < 4 else 4 * prompt_rows + block)

        def score(h, b):
            state = states[h]
            if b < 4:
                found = lax.dot_general(
                    jnp.concatenate([keys_p[b], hidden[r, b]], axis=1),
                    jnp.concatenate([queries[h], extra], axis=1),
                    contract,
                    preferred_element_type=jnp.float32,
                )
            else:
                found = lax.dot_general(
                    keys_c[own_keys, :], queries[h], contract, preferred_element_type=jnp.float32
                )
                found = jnp.where(lax.broadcasted_iota(jnp.int32, (block, block), 0) <= own_rows, found, -1e30)
            scores[h, span(b), :] = found
            highest = jnp.max(found.reshape(-1, 8, block), axis=0)
            state["max"] = jnp.maximum(state["max"], highest) if "max" in state else highest
            if b == 4:
                state["max"] = jnp.max(state["max"], axis=0, keepdims=True) * factor

        def weigh(h, b):
            state = states[h]
            chances = jnp.exp2(scores[h, span(b), :] * factor - state["max"])
            total = jnp.sum(chances.reshape(-1, 8, block), axis=0)
            values = values_p[b] if b < 4 else values_c[:, own_keys]
            mixed = jnp.dot(values, chances.astype(jnp.bfloat16), preferred_element_type=jnp.float32)
            state["sum"] = state["sum"] + total if "sum" in state else total
            state["mix"] = state["mix"] + mixed if "mix" in state else mixed

        def finish(h):
            state = states[h]
            result = jnp.transpose(state["mix"] / jnp.sum(state["sum"], axis=0, keepdims=True))
            write(h, jnp.where(valid, result, 0.0).astype(jnp.bfloat16))

        count = len(queries)
        for b in range(5):
            score(0, b)
        for h in range(count):
            for b in range(5):
                weigh(h, b)
                if h + 1 < count:
                    score(h + 1, b)
            finish(h)

    def projected(where, j):
        product = jnp.dot(acts[0, where, :], wts[j, :part, :], preferred_element_type=jnp.float32)
        for s in range(1, slices):
            product = product + jnp.dot(
                acts[s, where, :], wts[j, s * part : (s + 1) * part, :], preferred_element_type=jnp.float32
            )
        return product

    def keep_keys(first, count, product, cosine, sine):
        keys_c[pl.ds(first, count), :] = rotated(product[:, :HEAD] + kb_ref[...], cosine, sine).astype(jnp.bfloat16)
        turned = product[:, HEAD:] + vb_ref[...]
        for b in range(count // HEAD):
            values_c[:, pl.ds(pl.multiple_of(first + b * HEAD, HEAD), HEAD)] = jnp.transpose(
                turned[b * HEAD : (b + 1) * HEAD, :]
            ).astype(jnp.bfloat16)

    def queries_of(j, product, cosine, sine):
        found = []
        for h in range(2):
            value = product[:, h * HEAD : (h + 1) * HEAD] + qb_ref[j - 1, :, h * HEAD : (h + 1) * HEAD]
            found.append(rotated(value, cosine, sine).astype(jnp.bfloat16))
        return found

    def whole_unit(r, j):
        first = pl.multiple_of(r * block, block)
        where = pl.ds(first, block)
        product = projected(where, j)
        cosine, sine = cosines[where, :], sines[where, :]
        pl.when(j == 0)(lambda: keep_keys(first, block, product, cosine, sine))

        @pl.when(j > 0)
        def _():
            queries = queries_of(j, product, cosine, sine)

            def write(h, value):
                results[j - 1, where, h * HEAD : (h + 1) * HEAD] = value

            valid = lax.broadcasted_iota(jnp.int32, (block, HEAD), 0) < length_ref[joined * cands + r]
            attend_heads(r, lax.broadcasted_iota(jnp.int32, (block, block), 1), queries, valid, write)
            result_copy(r, j - 1).start()

    def half_unit(n, j):
        count = block // 2
        r = cands - 1
        offset = (n - r) * count
        first = pl.multiple_of(r * block + offset, count)
        where = pl.ds(first, count)
        product = projected(where, j)
        cosine, sine = cosines[where, :], sines[where, :]
        pl.when(j == 0)(lambda: keep_keys(first, count, product, cosine, sine))

        @pl.when(j > 0)
        def _():
            queries = jnp.concatenate(queries_of(j, product, cosine, sine), axis=0)

            def write(_h, value):
                for h in range(2):
                    results[j - 1, where, h * HEAD : (h + 1) * HEAD] = value[h * count : (h + 1) * count, :]

            def own_row(axis, shape):
                place = lax.broadcasted_iota(jnp.int32, shape, axis)
                return offset + jnp.where(place < count, place, place - count)

            valid = own_row(0, (block, HEAD)) < length_ref[joined * cands + r]
            attend_heads(r, own_row(1, (block, block)), [queries], valid, write)
            result_place(n, j - 1, where).start()

    plan = []

    def add(events, *units):
        for n, unit in enumerate(units):
            plan.append((events if n == 0 else [], unit))

    E, P, C, J = link_event, pass_piece, await_chunk, await_columns
    add([(E, 6), (P, 5), (C, 0), (J, 0), (await_prompt, 0)], (0, 0), (0, 1))
    add([(E, 7), (C, 1)], (1, 0))
    add([(P, 6)], (1, 1))
    add([(E, 8), (P, 7), (J, 1)], (0, 2), (1, 2))
    add([(E, 9), (P, 8), (P, 9), (E, 10), (C, 2)], (2, 0), (2, 1))
    add([(P, 10), (E, 11)], (2, 2))
    add([(P, 11), (J, 2)], (0, 3))
    add([(E, 12)], (1, 3))
    add([(E, 13)], (2, 3))
    add([(C, 3)], (3, 0), (3, 1))
    add([(E, 14)], (3, 2), (3, 3))
    add([(J, 3)], (0, 4))
    add([(E, 15)], (1, 4), (2, 4))
    add([(E, 16)], (3, 4))
    add([(C, 4)], (4, 0), (4, 1), (4, 2), (4, 3), (4, 4))

    def unit(u, _):
        for k, (events, _unit) in enumerate(plan):
            if events:

                @pl.when(u == k)
                def _():
                    for call, argument in events:
                        call(argument)

        r, j = 0, 0
        for k, (_events, (unit_r, unit_j)) in enumerate(plan):
            r = r + jnp.where(u == k, unit_r, 0)
            j = j + jnp.where(u == k, unit_j, 0)
        pl.when(r < cands - 1)(lambda: whole_unit(r, j))
        pl.when(r >= cands - 1)(lambda: half_unit(r, j))
        return 0

    lax.fori_loop(0, len(plan), unit, 0)

    for r in range(chunks):
        for j in range(columns):
            result_copy(r, j).wait()
    for n in range(3):
        for kind in range(2):
            prompt_copy(n, kind, joined).wait_send()
    for t in range(tps - 1):
        stat_copy(t).wait_send()
    for i in range(pieces + 1):
        direct(i).wait_send()
    for i in range(relayed):
        relay(i).wait_send()
    for r in range(chunks):
        to_sibling(tp, r).wait_send()
        pl.when(z < floors - 1)(lambda: own(r, 0).wait_send())
        pl.when(z > 0)(lambda: own(r, 1).wait_send())
        for f in range(floors):
            s = 2 * f + core

            @pl.when(z != f)
            def _():
                to_sibling(s, r).wait_send()

            @pl.when((f < z) & (z < floors - 1))
            def _():
                forward(s, r, up).wait_send()

            @pl.when((f > z) & (z > 0))
            def _():
                forward(s, r, down).wait_send()


def fits(prompt_inputs, cand_inputs, w_query, w_key):
    rows, part = cand_inputs.shape
    tps = lax.axis_size("tp")
    return (
        lax.axis_size("cache") == 2
        and lax.axis_size("cand") == 2
        and tps % 2 == 0
        and tps >= 4
        and rows == 4 * CLEN
        and w_key.shape[1] == HEAD
        and w_query.shape[1] == 8 * HEAD
        and part * tps == D
        and prompt_inputs.shape[0] % HEAD == 0
        and prompt_inputs.shape[0] <= 4 * HEAD
        and w_query.shape[0] == 4 * part
    )


def whole_layer(
    prompt_inputs,
    cand_inputs,
    norm_gain,
    w_query,
    w_key,
    w_value,
    q_bias,
    k_bias,
    v_bias,
    cand_lengths,
    prefix_ends,
):
    rows, part = cand_inputs.shape
    tps = lax.axis_size("tp")
    cands, wide = rows // CLEN, 2 * HEAD
    chunks = len(chunk_bounds(rows))
    columns = w_query.shape[1] // wide
    pieces = len(piece_table(columns, w_query.shape[0] // 2))
    prompt_rows = prompt_inputs.shape[0]
    half_freq = ROPE_THETA ** (-np.arange(HEAD // 2, dtype=np.float64) * 2.0 / HEAD)
    freq = jnp.asarray(np.concatenate([half_freq, half_freq]).astype(np.float32).reshape(1, HEAD))
    anywhere = pl.BlockSpec(memory_space=pl.ANY)
    vmem = pl.BlockSpec(memory_space=pltpu.VMEM)
    smem = pl.BlockSpec(memory_space=pltpu.SMEM)
    dma = pltpu.SemaphoreType.DMA
    return pl.pallas_call(
        layer_kernel,
        out_shape=jax.ShapeDtypeStruct((rows, columns * wide), jnp.bfloat16),
        in_specs=[anywhere, anywhere, vmem, anywhere, anywhere, anywhere, vmem, vmem, vmem, vmem, smem, smem],
        out_specs=anywhere,
        scratch_shapes=[
            pltpu.VMEM((tps, rows, part), jnp.bfloat16),
            pltpu.VMEM((1 + columns, part * tps, wide), jnp.bfloat16),
            pltpu.VMEM((prompt_rows, part * tps), jnp.bfloat16),
            pltpu.VMEM((rows, HEAD), jnp.float32),
            pltpu.VMEM((rows, HEAD), jnp.float32),
            pltpu.VMEM((tps, 1, rows), jnp.float32),
            pltpu.VMEM((4, prompt_rows, HEAD), jnp.bfloat16),
            pltpu.VMEM((4, HEAD, prompt_rows), jnp.bfloat16),
            pltpu.VMEM((rows, HEAD), jnp.bfloat16),
            pltpu.VMEM((HEAD, rows), jnp.bfloat16),
            pltpu.VMEM((cands, 4, prompt_rows, HEAD), jnp.bfloat16),
            pltpu.VMEM((2, 4 * prompt_rows + CLEN, CLEN), jnp.float32),
            pltpu.VMEM((columns, rows, wide), jnp.bfloat16),
            dma((4 + columns,)),
            dma((pieces + 1,)),
            dma((pieces + 1,)),
            dma((pieces,)),
            dma((pieces,)),
            dma((2, chunks)),
            dma((tps, chunks)),
            dma((tps, chunks)),
            dma((tps, chunks)),
            dma((tps - 1,)),
            dma((tps,)),
            dma((3, 2)),
            dma((3, 2)),
            dma((chunks, columns)),
        ],
        compiler_params=pltpu.CompilerParams(
            collective_id=0, has_side_effects=True, vmem_limit_bytes=64 * 1024 * 1024 - 65536
        ),
        name="whole_layer",
    )(
        cand_inputs.reshape(rows, part),
        prompt_inputs,
        norm_gain.reshape(tps, 1, part),
        w_query,
        w_key,
        w_value,
        q_bias.reshape(columns, 1, wide),
        k_bias.reshape(1, HEAD),
        v_bias.reshape(1, HEAD),
        freq,
        prefix_ends,
        cand_lengths,
    )


def query_product(normed, w_query):
    caches = lax.axis_size("cache")
    cands = lax.axis_size("cand")
    depth = w_query.shape[0]
    if caches != 2 or cands != 2 or depth % 4 != 0:
        return jnp.dot(
            normed,
            lax.all_gather(w_query, "cache", axis=0, tiled=True),
            preferred_element_type=jnp.float32,
        )
    mine = lax.axis_index("cache")
    side = lax.axis_index("cand")
    part = depth // 4
    swap = [(0, 1), (1, 0)]
    direct = [
        lax.ppermute(
            lax.dynamic_slice_in_dim(w_query, (2 * side + turn) * part, part), "cache", swap
        )
        for turn in range(2)
    ]
    relayed = [lax.ppermute(piece, "cand", swap) for piece in direct]

    def product(first, weights):
        columns = lax.dynamic_slice_in_dim(normed, first, weights.shape[0], 1)
        return jnp.dot(columns, weights, preferred_element_type=jnp.float32)

    total = product(mine * depth, w_query)
    other = (1 - mine) * depth
    for turn in range(2):
        total = total + product(other + (2 * side + turn) * part, direct[turn])
    for turn in range(2):
        total = total + product(other + (2 * (1 - side) + turn) * part, relayed[turn])
    return total


def per_device(
    prompt_inputs,
    cand_inputs,
    norm_gain,
    w_query,
    w_key,
    w_value,
    q_bias,
    k_bias,
    v_bias,
    cand_lengths,
    prefix_ends,
):
    prompt_dev = prompt_inputs.shape[0]
    cand_dev = cand_inputs.shape[0]
    head_size = HEAD
    kv_local = w_key.shape[1] // head_size
    groups = HEADS // KV_HEADS
    kv_width = kv_local * head_size
    joined = lax.axis_index("cache") * lax.axis_size("cand") + lax.axis_index("cand")
    if fits(prompt_inputs, cand_inputs, w_query, w_key):
        return whole_layer(
            prompt_inputs,
            cand_inputs,
            norm_gain,
            w_query,
            w_key,
            w_value,
            q_bias,
            k_bias,
            v_bias,
            cand_lengths,
            prefix_ends,
        )
    widened_p = prompt_inputs.astype(jnp.float32)
    normed_p = (
        widened_p
        * lax.rsqrt(jnp.mean(widened_p * widened_p, axis=-1, keepdims=True) + EPSILON)
        * norm_gain
    ).astype(jnp.bfloat16)
    widened_c = cand_inputs.astype(jnp.float32)
    squares = lax.psum(jnp.sum(widened_c * widened_c, axis=-1), "tp")
    part_width = cand_inputs.shape[1]
    gain_part = lax.dynamic_slice_in_dim(norm_gain, lax.axis_index("tp") * part_width, part_width)
    normed_part = (widened_c * lax.rsqrt(squares / D + EPSILON)[:, None] * gain_part).astype(
        jnp.bfloat16
    )
    normed_c = lax.all_gather(normed_part, "tp", axis=1, tiled=True)
    row_ids = joined * cand_dev + jnp.arange(cand_dev, dtype=jnp.int32)
    prefix_row = row_lookup(row_ids, prefix_ends)
    cand_pos = prefix_row + row_ids % CLEN
    prompt_pos = joined * prompt_dev + jnp.arange(prompt_dev, dtype=jnp.int32)
    key_value = jnp.concatenate([w_key, w_value], axis=1)
    if lax.axis_size("cache") == 2:
        other_half = lax.ppermute(key_value, "cache", [(0, 1), (1, 0)])
        key_value = jnp.where(
            lax.axis_index("cache") == 0,
            jnp.concatenate([key_value, other_half], axis=0),
            jnp.concatenate([other_half, key_value], axis=0),
        )
    else:
        key_value = lax.all_gather(key_value, "cache", axis=0, tiled=True)
    kv_prompt = jnp.dot(normed_p, key_value, preferred_element_type=jnp.float32)

    def keys_values(product, positions):
        rows = product.shape[0]
        keys = rotate(
            (product[:, :kv_width] + k_bias).reshape(rows, kv_local, head_size), positions
        ).astype(jnp.bfloat16)
        values = (product[:, kv_width:] + v_bias).astype(jnp.bfloat16)
        values = values.reshape(rows, kv_local, head_size)
        return jnp.concatenate([keys, values], axis=2).reshape(rows, 2 * kv_width)

    kv_p = lax.all_gather(
        keys_values(kv_prompt, prompt_pos), ("cache", "cand"), axis=0, tiled=True
    )
    q_cand = query_product(normed_c, w_query)
    kv_c = keys_values(jnp.dot(normed_c, key_value, preferred_element_type=jnp.float32), cand_pos)
    queries = rotate(
        (q_cand + q_bias).reshape(cand_dev, kv_local * groups, head_size), cand_pos
    ).astype(jnp.bfloat16)
    tile_rows = min(cand_dev, CLEN)
    tile_first = joined * cand_dev + tile_rows * jnp.arange(cand_dev // tile_rows, dtype=jnp.int32)
    prefixes = row_lookup(tile_first, prefix_ends)
    lengths = row_lookup(tile_first, cand_lengths)
    offsets = tile_first % CLEN
    if cand_dev < CLEN:
        kv_c = lax.all_gather(kv_c, ("cache", "cand"), axis=0, tiled=True)
        kv_c = lax.dynamic_slice_in_dim(kv_c, joined * cand_dev // CLEN * CLEN, CLEN)
    return attend(
        prefixes,
        lengths,
        offsets,
        queries.reshape(cand_dev, kv_local * groups * head_size),
        kv_p,
        kv_c,
        kv_local,
        groups,
    )


def solution(mesh):
    placed = (
        P(("cache", "cand"), None),
        P(("cache", "cand"), "tp"),
        P(),
        P("cache", "tp"),
        P("cache", "tp"),
        P("cache", "tp"),
        P("tp"),
        P("tp"),
        P("tp"),
        P(),
        P(),
    )
    return jax.shard_map(
        per_device,
        mesh=mesh,
        in_specs=placed,
        out_specs=P(("cache", "cand"), "tp"),
        check_vma=False,
    )
```

```python
import functools
import math

import jax
import jax.numpy as jnp
import numpy as np
from jax import lax
from jax.experimental import pallas as pl
from jax.experimental.pallas import tpu as pltpu
from jax.sharding import PartitionSpec as P

D = 8192
HEADS = 64
KV_HEADS = 8
HEAD = 128
CANDS = 16
CLEN = 256


ROPE_THETA = 1000000.0
EPSILON = 1e-06


def rotate(tensor, positions):
    half_size = tensor.shape[-1] // 2
    inverse_freq = jnp.power(
        ROPE_THETA, -jnp.arange(half_size, dtype=jnp.float32) * 2.0 / tensor.shape[-1]
    )
    angles = positions.astype(jnp.float32)[:, None] * inverse_freq[None, :]
    cosine = jnp.cos(angles)[:, None, :]
    sine_part = jnp.sin(angles)[:, None, :]
    first_half = tensor[..., :half_size]
    second = tensor[..., half_size:]
    return jnp.concatenate(
        [first_half * cosine - second * sine_part, second * cosine + first_half * sine_part],
        axis=-1,
    )


def row_lookup(row_ids, table):
    chosen = (row_ids // CLEN)[:, None] == jnp.arange(CANDS, dtype=jnp.int32)[None, :]
    return jnp.sum(jnp.where(chosen, table[None, :], 0), axis=1)


def attend_kernel(
    prefix_ref, length_ref, offset_ref, q_ref, kvp_ref, kvc_ref, out_ref, *, heads, chunk, scale
):
    cand = pl.program_id(0)
    prefix = prefix_ref[cand]
    length = length_ref[cand]
    offset = offset_ref[cand]
    rows = q_ref.shape[0]
    contract = (((1,), (1,)), ((), ()))

    def scores_of(head, key_rows):
        return (
            lax.dot_general(
                q_ref[:, head * HEAD : (head + 1) * HEAD],
                key_rows,
                contract,
                preferred_element_type=jnp.float32,
            )
            * scale
        )

    def weighted(probabilities, value_rows):
        return jnp.dot(
            probabilities.astype(jnp.bfloat16), value_rows, preferred_element_type=jnp.float32
        )

    own_shape = (rows, kvc_ref.shape[0])
    causal = lax.broadcasted_iota(jnp.int32, own_shape, 1) <= offset + lax.broadcasted_iota(
        jnp.int32, own_shape, 0
    )
    state = []
    for head in range(heads):
        scores = jnp.where(causal, scores_of(head, kvc_ref[:, :HEAD]), -1e30)
        maxima = jnp.max(scores, axis=1, keepdims=True)
        probabilities = jnp.exp2(scores - maxima)
        totals = jnp.sum(probabilities, axis=1, keepdims=True)
        state += [maxima, totals, weighted(probabilities, kvc_ref[:, HEAD:])]

    def advance(turn, running):
        first = pl.multiple_of(turn * chunk, chunk)
        key_rows = kvp_ref[pl.ds(first, chunk), :HEAD]
        value_rows = kvp_ref[pl.ds(first, chunk), HEAD:]
        seen = first + lax.broadcasted_iota(jnp.int32, (rows, chunk), 1) < prefix
        following = []
        for head in range(heads):
            maxima, totals, accumulated = running[3 * head : 3 * head + 3]
            scores = jnp.where(seen, scores_of(head, key_rows), -1e30)
            new_maxima = jnp.maximum(maxima, jnp.max(scores, axis=1, keepdims=True))
            probabilities = jnp.exp2(scores - new_maxima)
            rescale = jnp.exp2(maxima - new_maxima)
            totals = totals * rescale + jnp.sum(probabilities, axis=1, keepdims=True)
            accumulated = accumulated * rescale + weighted(probabilities, value_rows)
            following += [new_maxima, totals, accumulated]
        return tuple(following)

    state = lax.fori_loop(0, (prefix + chunk - 1) // chunk, advance, tuple(state))
    valid = offset + lax.broadcasted_iota(jnp.int32, (rows, HEAD), 0) < length
    for head in range(heads):
        result = state[3 * head + 2] / state[3 * head + 1]
        out_ref[:, head * HEAD : (head + 1) * HEAD] = jnp.where(valid, result, 0.0).astype(
            jnp.bfloat16
        )


def attend(prefixes, lengths, offsets, queries, kv_prompt, kv_cand, kv_local, groups):
    tiles = prefixes.shape[0]
    rows = queries.shape[0] // tiles
    prompt = kv_prompt.shape[0]
    chunk = next(size for size in (512, 256, 128, prompt) if prompt % size == 0)
    heads = 2 if groups % 2 == 0 else 1
    turns = groups // heads
    return pl.pallas_call(
        functools.partial(
            attend_kernel, heads=heads, chunk=chunk, scale=HEAD ** (-0.5) * math.log2(math.e)
        ),
        grid_spec=pltpu.PrefetchScalarGridSpec(
            num_scalar_prefetch=3,
            grid=(tiles, kv_local, turns),
            in_specs=[
                pl.BlockSpec((rows, heads * HEAD), lambda c, k, t, *_: (c, k * turns + t)),
                pl.BlockSpec((prompt, 2 * HEAD), lambda c, k, t, *_: (0, k)),
                pl.BlockSpec((CLEN, 2 * HEAD), lambda c, k, t, *_: (c, k)),
            ],
            out_specs=pl.BlockSpec((rows, heads * HEAD), lambda c, k, t, *_: (c, k * turns + t)),
        ),
        out_shape=jax.ShapeDtypeStruct(queries.shape, jnp.bfloat16),
        cost_estimate=pl.CostEstimate(
            flops=4 * queries.size * (prompt + CLEN),
            bytes_accessed=4 * queries.size,
            transcendentals=queries.size // HEAD * (prompt + CLEN),
        ),
        compiler_params=pltpu.CompilerParams(vmem_limit_bytes=60 * 1024 * 1024),
    )(prefixes, lengths, offsets, queries, kv_prompt, kv_cand)


MESH = pl.DeviceIdType.MESH


EXTRA = 2


def chunk_bounds(rows):
    whole = [(first, CLEN) for first in range(0, rows - CLEN, CLEN)]
    return whole + [(rows - CLEN, CLEN // 2), (rows - CLEN // 2, CLEN // 2)]


def piece_table(columns, quarter):
    table = [(0, 0, 0, quarter // 2), (0, 0, quarter // 2, quarter // 2), (0, 1, 0, quarter)]
    for j in range(columns):
        count = 2 if j < columns - 1 else 4
        table += [(1 + j, None, n * (quarter // count), quarter // count) for n in range(count)]
    return table


def link_orders(depths, chunks):
    orders = [[(0, r) for r in range(chunks)]]
    for depth in range(1, depths):
        ready = {(d + 1, r): k + 2 for k, (d, r) in enumerate(orders[-1])}
        ready.update({(0, r): 0 for r in range(chunks)})
        order = []
        while ready:
            slot = len(order)
            able = [e for e in ready if ready[e] <= slot] or list(ready)
            pick = min(able, key=lambda e: (e[1], e[0]))
            del ready[pick]
            order.append(pick)
        orders.append(order)
    return orders


def layer_kernel(
    xc_ref, xp_ref, gain_ref, wq_ref, wk_ref, wv_ref, qb_ref, kb_ref, vb_ref, freq_ref, prefix_ref, length_ref,
    out_ref,
    acts, wts, prompt, cosines, sines, stats, keys_p, values_p, keys_c, values_c, hidden, scores, results,
    load_sem, wsend, wrecv, rsend, rrecv, own_sem, fwd_sem, sib_sem, arr_sem, st_send, st_recv, kp_send, kp_recv, out_sem,
):
    y, tp, x = lax.axis_index("cache"), lax.axis_index("tp"), lax.axis_index("cand")
    tps = lax.axis_size("tp")
    floors = tps // 2
    z, core = tp // 2, tp % 2
    rows, part = xc_ref.shape
    block = CLEN
    cands = rows // block
    bounds = chunk_bounds(rows)
    chunks = len(bounds)
    half = wq_ref.shape[0]
    quarter = half // 2
    wide = 2 * HEAD
    columns = wq_ref.shape[1] // wide
    table_of_pieces = piece_table(columns, quarter)
    pieces = len(table_of_pieces)
    prompt_rows = xp_ref.shape[0]
    slices = tps
    joined = y * 2 + x

    up, down, sib = (y, tp + 2, x), (y, tp - 2, x), (y, tp + 1 - 2 * core, x)
    over, aside, across = (1 - y, tp, x), (y, tp, 1 - x), (1 - y, tp, 1 - x)
    peers = [(y, (tp + t) % tps, x) for t in range(1, tps)]

    barrier = pltpu.get_barrier_semaphore()
    for peer in peers + [over, aside, across]:
        pl.semaphore_signal(barrier, inc=1, device_id=peer, device_id_type=MESH)

    load_x = pltpu.make_async_copy(xc_ref, acts.at[tp], load_sem.at[0])
    load_p = pltpu.make_async_copy(xp_ref, prompt, load_sem.at[1])
    own_rows = pl.ds(pl.multiple_of(y * half, half), half)
    load_w = [
        pltpu.make_async_copy(wk_ref, wts.at[0, own_rows, :HEAD], load_sem.at[2]),
        pltpu.make_async_copy(wv_ref, wts.at[0, own_rows, HEAD:], load_sem.at[3]),
    ] + [
        pltpu.make_async_copy(
            wq_ref.at[:, j * wide : (j + 1) * wide], wts.at[1 + j, own_rows, :], load_sem.at[4 + j]
        )
        for j in range(columns)
    ]
    load_x.start()
    load_p.start()
    for copy in load_w:
        copy.start()

    def piece_place(i, side_y, side_x):
        j, side, first, count = table_of_pieces[i]
        where = pl.ds(pl.multiple_of(side_y * half + side_x * quarter + first, count), count)
        return wts.at[0, where, side * HEAD : (side + 1) * HEAD] if j == 0 else wts.at[j, where, :]

    relayed = pieces - EXTRA

    def direct(n):
        i, side_x = (n, x) if n < pieces else (n - EXTRA, 1 - x)
        j, side, first, count = table_of_pieces[i]
        where = pl.ds(pl.multiple_of(side_x * quarter + first, count), count)
        src = (wk_ref, wv_ref)[side].at[where, :] if j == 0 else wq_ref.at[where, (j - 1) * wide : j * wide]
        return pltpu.make_async_remote_copy(
            src_ref=src, dst_ref=piece_place(i, y, side_x), send_sem=wsend.at[n], recv_sem=wrecv.at[n],
            device_id=over, device_id_type=MESH,
        )

    def relay(i):
        place = piece_place(i, 1 - y, x)
        return pltpu.make_async_remote_copy(
            src_ref=place, dst_ref=place, send_sem=rsend.at[i], recv_sem=rrecv.at[i],
            device_id=aside, device_id_type=MESH,
        )

    def pass_piece(i):
        direct(i).wait_recv()
        relay(i).start()

    def send_piece(i):
        direct(i).start()

    def slab(s, r):
        return acts.at[s, pl.ds(*bounds[r]), :]

    def slab_copy(s, r, send, target):
        return pltpu.make_async_remote_copy(
            src_ref=slab(s, r), dst_ref=slab(s, r), send_sem=send, recv_sem=arr_sem.at[s, r],
            device_id=target, device_id_type=MESH,
        )

    def to_sibling(s, r):
        return slab_copy(s, r, sib_sem.at[s, r], sib)

    def forward(s, r, target):
        return slab_copy(s, r, fwd_sem.at[s, r], target)

    def own(r, way):
        return slab_copy(tp, r, own_sem.at[way, r], (up, down)[way])

    orders = link_orders(floors - 1, chunks)
    longest = orders[-1]

    def link_event(k):
        if 0 <= k - 2 < len(longest):
            distance, r = longest[k - 2]

            @pl.when(z == 0)
            def _():
                s = tp + 2 * (distance + 1)
                forward(s, r, down).wait_recv()
                to_sibling(s, r).start()

            @pl.when(z == floors - 1)
            def _():
                s = tp - 2 * (distance + 1)
                forward(s, r, up).wait_recv()
                to_sibling(s, r).start()

        for depth, order in enumerate(orders):
            if k >= len(order):
                continue
            distance, r = order[k]

            def go(way, sign, target):
                if distance == 0:
                    own(r, way).start()
                else:
                    s = tp + sign * 2 * distance
                    copy = forward(s, r, target)
                    copy.wait_recv()
                    copy.start()
                    to_sibling(s, r).start()

            pl.when(z == depth)(functools.partial(go, 0, -1, up))
            pl.when(floors - 1 - z == depth)(functools.partial(go, 1, 1, down))

    pl.semaphore_wait(barrier, tps + 2)
    for i in range(5):
        send_piece(i)

    load_x.wait()
    for r in range(cands):
        wide_x = acts[tp, pl.ds(r * block, block), :].astype(jnp.float32)
        squares = wide_x * wide_x
        lanes = squares[:, :HEAD]
        for t in range(1, part // HEAD):
            lanes = lanes + squares[:, t * HEAD : (t + 1) * HEAD]
        for b in range(block // HEAD):
            turned = jnp.transpose(lanes[b * HEAD : (b + 1) * HEAD, :])
            stats[tp, :, pl.ds(r * block + b * HEAD, HEAD)] = jnp.sum(turned, axis=0, keepdims=True)

    def stat_copy(t):
        return pltpu.make_async_remote_copy(
            src_ref=stats.at[tp], dst_ref=stats.at[tp], send_sem=st_send.at[t], recv_sem=st_recv.at[tp],
            device_id=peers[t], device_id_type=MESH,
        )

    def stat_arrival(t):
        s = (tp + 1 + t) % tps
        return pltpu.make_async_remote_copy(
            src_ref=stats.at[s], dst_ref=stats.at[s], send_sem=st_send.at[t], recv_sem=st_recv.at[s],
            device_id=peers[t], device_id_type=MESH,
        )

    for t in range(tps - 1):
        stat_copy(t).start()
    for t in range(tps - 1):
        stat_arrival(t).wait_recv()
    total = stats[0]
    for s in range(1, tps):
        total = total + stats[s]
    inverse = lax.rsqrt(total / (part * tps) + EPSILON)

    for r in range(cands):
        line = jnp.broadcast_to(inverse[:, r * block : (r + 1) * block], (HEAD, block))
        column = jnp.concatenate(
            [jnp.transpose(line[:, b * HEAD : (b + 1) * HEAD]) for b in range(block // HEAD)], axis=0
        )
        column = jnp.concatenate([column] * (part // HEAD), axis=1)
        place = (tp, pl.ds(r * block, block), slice(None))
        acts[place] = (acts[place].astype(jnp.float32) * column * gain_ref[tp]).astype(jnp.bfloat16)
        if r == 1:
            link_event(0)
        if r >= 1:
            to_sibling(tp, r - 1).start()
    link_event(1)
    for r in range(cands - 1, chunks):
        to_sibling(tp, r).start()

    lane = lax.broadcasted_iota(jnp.int32, (1, HEAD), 1)
    sign = jnp.where(lane < HEAD // 2, -1.0, 1.0)

    def table(first, count):
        place = first + lax.broadcasted_iota(jnp.int32, (count, HEAD), 0)
        angles = place.astype(jnp.float32) * freq_ref[...]
        return jnp.cos(angles), jnp.sin(angles) * sign

    def fill(b, _):
        start = pl.multiple_of(b * HEAD, HEAD)
        cand = joined * cands + b // (block // HEAD)
        cosines[pl.ds(start, HEAD), :], sines[pl.ds(start, HEAD), :] = table(
            prefix_ref[cand] + b % (block // HEAD) * HEAD, HEAD
        )
        return 0

    lax.fori_loop(0, rows // HEAD, fill, 0)

    def hide(n, _):
        r, b = n // 4, n % 4
        key = b * prompt_rows + lax.broadcasted_iota(jnp.int32, (prompt_rows, HEAD), 0)
        first = lax.broadcasted_iota(jnp.int32, (prompt_rows, HEAD), 1) == 0
        unseen = first & (key >= prefix_ref[joined * cands + r])
        hidden[r, b] = jnp.where(unseen, -1e30, 0.0).astype(jnp.bfloat16)
        return 0

    lax.fori_loop(0, 4 * cands, hide, 0)
    later = pl.ds(*bounds[-1])
    keys_c[later, :] = jnp.zeros((bounds[-1][1], HEAD), jnp.bfloat16)
    values_c[:, later] = jnp.zeros((HEAD, bounds[-1][1]), jnp.bfloat16)

    def rotated(value, cosine, sine):
        return value * cosine + pltpu.roll(value, HEAD // 2, 1) * sine

    pass_piece(0)
    pass_piece(1)
    link_event(2)

    load_p.wait()
    slab_rows = 32

    def norm_prompt(b, _):
        where = pl.ds(pl.multiple_of(b * slab_rows, slab_rows), slab_rows)
        squares = jnp.zeros((slab_rows, 1), jnp.float32)
        for s in range(slices):
            value = prompt[where, s * part : (s + 1) * part].astype(jnp.float32)
            squares = squares + jnp.sum(value * value, axis=1, keepdims=True)
        scale = lax.rsqrt(squares / (part * slices) + EPSILON)
        for s in range(slices):
            value = prompt[where, s * part : (s + 1) * part].astype(jnp.float32)
            prompt[where, s * part : (s + 1) * part] = (value * scale * gain_ref[s]).astype(jnp.bfloat16)
        return 0

    lax.fori_loop(0, prompt_rows // slab_rows, norm_prompt, 0)
    pass_piece(2)
    link_event(3)
    pass_piece(3)
    link_event(4)

    def await_piece(i):
        place = piece_place(i, 1 - y, 1 - x)
        pltpu.make_async_remote_copy(
            src_ref=place, dst_ref=place, send_sem=rsend.at[i], recv_sem=rrecv.at[i],
            device_id=aside, device_id_type=MESH,
        ).wait_recv()

    load_w[0].wait()
    load_w[1].wait()
    for i in range(3):
        await_piece(i)

    def prompt_block(b, _):
        where = pl.ds(pl.multiple_of(b * HEAD, HEAD), HEAD)
        product = jnp.dot(prompt[where, :part], wts[0, :part, :], preferred_element_type=jnp.float32)
        for s in range(1, slices):
            product = product + jnp.dot(
                prompt[where, s * part : (s + 1) * part],
                wts[0, s * part : (s + 1) * part, :],
                preferred_element_type=jnp.float32,
            )
        cosine, sine = table(joined * prompt_rows + b * HEAD, HEAD)
        keys_p[joined, where, :] = rotated(product[:, :HEAD] + kb_ref[...], cosine, sine).astype(jnp.bfloat16)
        values_p[joined, :, where] = jnp.transpose(product[:, HEAD:] + vb_ref[...]).astype(jnp.bfloat16)
        return 0

    lax.fori_loop(0, prompt_rows // HEAD, prompt_block, 0)

    def prompt_copy(n, kind, slot):
        place = (keys_p, values_p)[kind].at[slot]
        return pltpu.make_async_remote_copy(
            src_ref=place, dst_ref=place, send_sem=kp_send.at[n, kind], recv_sem=kp_recv.at[n, kind],
            device_id=(over, aside, across)[n], device_id_type=MESH,
        )

    for n in range(3):
        for kind in range(2):
            prompt_copy(n, kind, joined).start()
    for i in range(5, 8):
        send_piece(i)
    pass_piece(4)
    link_event(5)
    for i in range(8, pieces + EXTRA):
        send_piece(i)

    def await_columns(j):
        load_w[2 + j].wait()
        for i in range(pieces):
            if table_of_pieces[i][0] == 1 + j and i < relayed:
                await_piece(i)
        if j == columns - 1:
            for i in range(relayed, pieces + EXTRA):
                direct(i).wait_recv()

    def await_chunk(r):
        for f in range(floors):
            to_sibling(2 * f + 1 - core, r).wait_recv()

    def await_prompt(_):
        for n, slot in enumerate(((1 - y) * 2 + x, y * 2 + 1 - x, (1 - y) * 2 + 1 - x)):
            for kind in range(2):
                prompt_copy(n, kind, slot).wait_recv()

    def result_copy(n, j):
        where = pl.ds(*bounds[n]) if isinstance(n, int) else pl.ds(pl.multiple_of(n * block, block), block)
        return result_place(n, j, where)

    def result_place(n, j, where):
        across_columns = pl.ds(pl.multiple_of(j * wide, wide), wide)
        return pltpu.make_async_copy(
            results.at[j, where, :], out_ref.at[where, across_columns], out_sem.at[n, j]
        )

    factor = HEAD ** (-0.5) * math.log2(math.e)

    def attend_heads(r, own_rows, queries, valid, write):
        extra = jnp.where(lax.broadcasted_iota(jnp.int32, (block, HEAD), 1) == 0, 1.0, 0.0).astype(jnp.bfloat16)
        own_keys = pl.ds(pl.multiple_of(r * block, block), block)
        contract = (((1,), (1,)), ((), ()))
        states = [{} for _ in queries]

        def span(b):
            return slice(b * prompt_rows, (b + 1) * prompt_rows if b < 4 else 4 * prompt_rows + block)

        def score(h, b):
            state = states[h]
            if b < 4:
                found = lax.dot_general(
                    jnp.concatenate([keys_p[b], hidden[r, b]], axis=1),
                    jnp.concatenate([queries[h], extra], axis=1),
                    contract,
                    preferred_element_type=jnp.float32,
                )
            else:
                found = lax.dot_general(
                    keys_c[own_keys, :], queries[h], contract, preferred_element_type=jnp.float32
                )
                found = jnp.where(lax.broadcasted_iota(jnp.int32, (block, block), 0) <= own_rows, found, -1e30)
            scores[h, span(b), :] = found
            highest = jnp.max(found.reshape(-1, 8, block), axis=0)
            state["max"] = jnp.maximum(state["max"], highest) if "max" in state else highest
            if b == 4:
                state["max"] = jnp.max(state["max"], axis=0, keepdims=True) * factor

        def weigh(h, b):
            state = states[h]
            chances = jnp.exp2(scores[h, span(b), :] * factor - state["max"])
            total = jnp.sum(chances.reshape(-1, 8, block), axis=0)
            values = values_p[b] if b < 4 else values_c[:, own_keys]
            mixed = jnp.dot(values, chances.astype(jnp.bfloat16), preferred_element_type=jnp.float32)
            state["sum"] = state["sum"] + total if "sum" in state else total
            state["mix"] = state["mix"] + mixed if "mix" in state else mixed

        def finish(h):
            state = states[h]
            result = jnp.transpose(state["mix"] / jnp.sum(state["sum"], axis=0, keepdims=True))
            write(h, jnp.where(valid, result, 0.0).astype(jnp.bfloat16))

        count = len(queries)
        for b in range(5):
            score(0, b)
        for h in range(count):
            for b in range(5):
                weigh(h, b)
                if h + 1 < count:
                    score(h + 1, b)
            finish(h)

    def projected(where, j):
        product = jnp.dot(acts[0, where, :], wts[j, :part, :], preferred_element_type=jnp.float32)
        for s in range(1, slices):
            product = product + jnp.dot(
                acts[s, where, :], wts[j, s * part : (s + 1) * part, :], preferred_element_type=jnp.float32
            )
        return product

    def keep_keys(first, count, product, cosine, sine):
        keys_c[pl.ds(first, count), :] = rotated(product[:, :HEAD] + kb_ref[...], cosine, sine).astype(jnp.bfloat16)
        turned = product[:, HEAD:] + vb_ref[...]
        for b in range(count // HEAD):
            values_c[:, pl.ds(pl.multiple_of(first + b * HEAD, HEAD), HEAD)] = jnp.transpose(
                turned[b * HEAD : (b + 1) * HEAD, :]
            ).astype(jnp.bfloat16)

    def queries_of(j, product, cosine, sine):
        found = []
        for h in range(2):
            value = product[:, h * HEAD : (h + 1) * HEAD] + qb_ref[j - 1, :, h * HEAD : (h + 1) * HEAD]
            found.append(rotated(value, cosine, sine).astype(jnp.bfloat16))
        return found

    def whole_unit(r, j):
        first = pl.multiple_of(r * block, block)
        where = pl.ds(first, block)
        product = projected(where, j)
        cosine, sine = cosines[where, :], sines[where, :]
        pl.when(j == 0)(lambda: keep_keys(first, block, product, cosine, sine))

        @pl.when(j > 0)
        def _():
            queries = queries_of(j, product, cosine, sine)

            def write(h, value):
                results[j - 1, where, h * HEAD : (h + 1) * HEAD] = value

            valid = lax.broadcasted_iota(jnp.int32, (block, HEAD), 0) < length_ref[joined * cands + r]
            attend_heads(r, lax.broadcasted_iota(jnp.int32, (block, block), 1), queries, valid, write)
            result_copy(r, j - 1).start()

    def half_unit(n, j):
        count = block // 2
        r = cands - 1
        offset = (n - r) * count
        first = pl.multiple_of(r * block + offset, count)
        where = pl.ds(first, count)
        product = projected(where, j)
        cosine, sine = cosines[where, :], sines[where, :]
        pl.when(j == 0)(lambda: keep_keys(first, count, product, cosine, sine))

        @pl.when(j > 0)
        def _():
            queries = jnp.concatenate(queries_of(j, product, cosine, sine), axis=0)

            def write(_h, value):
                for h in range(2):
                    results[j - 1, where, h * HEAD : (h + 1) * HEAD] = value[h * count : (h + 1) * count, :]

            def own_row(axis, shape):
                place = lax.broadcasted_iota(jnp.int32, shape, axis)
                return offset + jnp.where(place < count, place, place - count)

            valid = own_row(0, (block, HEAD)) < length_ref[joined * cands + r]
            attend_heads(r, own_row(1, (block, block)), [queries], valid, write)
            result_place(n, j - 1, where).start()

    plan = []

    def add(events, *units):
        for n, unit in enumerate(units):
            plan.append((events if n == 0 else [], unit))

    E, P, C, J = link_event, pass_piece, await_chunk, await_columns
    add([(E, 6), (P, 5), (C, 0), (J, 0), (await_prompt, 0)], (0, 0), (0, 1))
    add([(E, 7), (C, 1)], (1, 0))
    add([(P, 6)], (1, 1))
    add([(E, 8), (P, 7), (J, 1)], (0, 2), (1, 2))
    add([(E, 9), (P, 8), (P, 9), (E, 10), (C, 2)], (2, 0), (2, 1))
    add([(P, 10), (E, 11)], (2, 2))
    add([(J, 2)], (0, 3))
    add([(E, 12)], (1, 3))
    add([(E, 13)], (2, 3))
    add([(C, 3)], (3, 0), (3, 1))
    add([(E, 14)], (3, 2), (3, 3))
    add([(J, 3)], (0, 4))
    add([(E, 15)], (1, 4), (2, 4))
    add([(E, 16)], (3, 4))
    add([(C, 4)], (4, 0), (4, 1), (4, 2), (4, 3), (4, 4))

    def unit(u, _):
        for k, (events, _unit) in enumerate(plan):
            if events:

                @pl.when(u == k)
                def _():
                    for call, argument in events:
                        call(argument)

        r, j = 0, 0
        for k, (_events, (unit_r, unit_j)) in enumerate(plan):
            r = r + jnp.where(u == k, unit_r, 0)
            j = j + jnp.where(u == k, unit_j, 0)
        pl.when(r < cands - 1)(lambda: whole_unit(r, j))
        pl.when(r >= cands - 1)(lambda: half_unit(r, j))
        return 0

    lax.fori_loop(0, len(plan), unit, 0)

    for r in range(chunks):
        for j in range(columns):
            result_copy(r, j).wait()
    for n in range(3):
        for kind in range(2):
            prompt_copy(n, kind, joined).wait_send()
    for t in range(tps - 1):
        stat_copy(t).wait_send()
    for i in range(pieces + EXTRA):
        direct(i).wait_send()
    for i in range(relayed):
        relay(i).wait_send()
    for r in range(chunks):
        to_sibling(tp, r).wait_send()
        pl.when(z < floors - 1)(lambda: own(r, 0).wait_send())
        pl.when(z > 0)(lambda: own(r, 1).wait_send())
        for f in range(floors):
            s = 2 * f + core

            @pl.when(z != f)
            def _():
                to_sibling(s, r).wait_send()

            @pl.when((f < z) & (z < floors - 1))
            def _():
                forward(s, r, up).wait_send()

            @pl.when((f > z) & (z > 0))
            def _():
                forward(s, r, down).wait_send()


def fits(prompt_inputs, cand_inputs, w_query, w_key):
    rows, part = cand_inputs.shape
    tps = lax.axis_size("tp")
    return (
        lax.axis_size("cache") == 2
        and lax.axis_size("cand") == 2
        and tps % 2 == 0
        and tps >= 4
        and rows == 4 * CLEN
        and w_key.shape[1] == HEAD
        and w_query.shape[1] == 8 * HEAD
        and part * tps == D
        and prompt_inputs.shape[0] % HEAD == 0
        and prompt_inputs.shape[0] <= 4 * HEAD
        and w_query.shape[0] == 4 * part
    )


def whole_layer(
    prompt_inputs,
    cand_inputs,
    norm_gain,
    w_query,
    w_key,
    w_value,
    q_bias,
    k_bias,
    v_bias,
    cand_lengths,
    prefix_ends,
):
    rows, part = cand_inputs.shape
    tps = lax.axis_size("tp")
    cands, wide = rows // CLEN, 2 * HEAD
    chunks = len(chunk_bounds(rows))
    columns = w_query.shape[1] // wide
    pieces = len(piece_table(columns, w_query.shape[0] // 2))
    prompt_rows = prompt_inputs.shape[0]
    half_freq = ROPE_THETA ** (-np.arange(HEAD // 2, dtype=np.float64) * 2.0 / HEAD)
    freq = jnp.asarray(np.concatenate([half_freq, half_freq]).astype(np.float32).reshape(1, HEAD))
    anywhere = pl.BlockSpec(memory_space=pl.ANY)
    vmem = pl.BlockSpec(memory_space=pltpu.VMEM)
    smem = pl.BlockSpec(memory_space=pltpu.SMEM)
    dma = pltpu.SemaphoreType.DMA
    return pl.pallas_call(
        layer_kernel,
        out_shape=jax.ShapeDtypeStruct((rows, columns * wide), jnp.bfloat16),
        in_specs=[anywhere, anywhere, vmem, anywhere, anywhere, anywhere, vmem, vmem, vmem, vmem, smem, smem],
        out_specs=anywhere,
        scratch_shapes=[
            pltpu.VMEM((tps, rows, part), jnp.bfloat16),
            pltpu.VMEM((1 + columns, part * tps, wide), jnp.bfloat16),
            pltpu.VMEM((prompt_rows, part * tps), jnp.bfloat16),
            pltpu.VMEM((rows, HEAD), jnp.float32),
            pltpu.VMEM((rows, HEAD), jnp.float32),
            pltpu.VMEM((tps, 1, rows), jnp.float32),
            pltpu.VMEM((4, prompt_rows, HEAD), jnp.bfloat16),
            pltpu.VMEM((4, HEAD, prompt_rows), jnp.bfloat16),
            pltpu.VMEM((rows, HEAD), jnp.bfloat16),
            pltpu.VMEM((HEAD, rows), jnp.bfloat16),
            pltpu.VMEM((cands, 4, prompt_rows, HEAD), jnp.bfloat16),
            pltpu.VMEM((2, 4 * prompt_rows + CLEN, CLEN), jnp.float32),
            pltpu.VMEM((columns, rows, wide), jnp.bfloat16),
            dma((4 + columns,)),
            dma((pieces + EXTRA,)),
            dma((pieces + EXTRA,)),
            dma((pieces,)),
            dma((pieces,)),
            dma((2, chunks)),
            dma((tps, chunks)),
            dma((tps, chunks)),
            dma((tps, chunks)),
            dma((tps - 1,)),
            dma((tps,)),
            dma((3, 2)),
            dma((3, 2)),
            dma((chunks, columns)),
        ],
        compiler_params=pltpu.CompilerParams(
            collective_id=0, has_side_effects=True, vmem_limit_bytes=64 * 1024 * 1024 - 65536
        ),
        name="whole_layer",
    )(
        cand_inputs.reshape(rows, part),
        prompt_inputs,
        norm_gain.reshape(tps, 1, part),
        w_query,
        w_key,
        w_value,
        q_bias.reshape(columns, 1, wide),
        k_bias.reshape(1, HEAD),
        v_bias.reshape(1, HEAD),
        freq,
        prefix_ends,
        cand_lengths,
    )


def query_product(normed, w_query):
    caches = lax.axis_size("cache")
    cands = lax.axis_size("cand")
    depth = w_query.shape[0]
    if caches != 2 or cands != 2 or depth % 4 != 0:
        return jnp.dot(
            normed,
            lax.all_gather(w_query, "cache", axis=0, tiled=True),
            preferred_element_type=jnp.float32,
        )
    mine = lax.axis_index("cache")
    side = lax.axis_index("cand")
    part = depth // 4
    swap = [(0, 1), (1, 0)]
    direct = [
        lax.ppermute(
            lax.dynamic_slice_in_dim(w_query, (2 * side + turn) * part, part), "cache", swap
        )
        for turn in range(2)
    ]
    relayed = [lax.ppermute(piece, "cand", swap) for piece in direct]

    def product(first, weights):
        columns = lax.dynamic_slice_in_dim(normed, first, weights.shape[0], 1)
        return jnp.dot(columns, weights, preferred_element_type=jnp.float32)

    total = product(mine * depth, w_query)
    other = (1 - mine) * depth
    for turn in range(2):
        total = total + product(other + (2 * side + turn) * part, direct[turn])
    for turn in range(2):
        total = total + product(other + (2 * (1 - side) + turn) * part, relayed[turn])
    return total


def per_device(
    prompt_inputs,
    cand_inputs,
    norm_gain,
    w_query,
    w_key,
    w_value,
    q_bias,
    k_bias,
    v_bias,
    cand_lengths,
    prefix_ends,
):
    prompt_dev = prompt_inputs.shape[0]
    cand_dev = cand_inputs.shape[0]
    head_size = HEAD
    kv_local = w_key.shape[1] // head_size
    groups = HEADS // KV_HEADS
    kv_width = kv_local * head_size
    joined = lax.axis_index("cache") * lax.axis_size("cand") + lax.axis_index("cand")
    if fits(prompt_inputs, cand_inputs, w_query, w_key):
        return whole_layer(
            prompt_inputs,
            cand_inputs,
            norm_gain,
            w_query,
            w_key,
            w_value,
            q_bias,
            k_bias,
            v_bias,
            cand_lengths,
            prefix_ends,
        )
    widened_p = prompt_inputs.astype(jnp.float32)
    normed_p = (
        widened_p
        * lax.rsqrt(jnp.mean(widened_p * widened_p, axis=-1, keepdims=True) + EPSILON)
        * norm_gain
    ).astype(jnp.bfloat16)
    widened_c = cand_inputs.astype(jnp.float32)
    squares = lax.psum(jnp.sum(widened_c * widened_c, axis=-1), "tp")
    part_width = cand_inputs.shape[1]
    gain_part = lax.dynamic_slice_in_dim(norm_gain, lax.axis_index("tp") * part_width, part_width)
    normed_part = (widened_c * lax.rsqrt(squares / D + EPSILON)[:, None] * gain_part).astype(
        jnp.bfloat16
    )
    normed_c = lax.all_gather(normed_part, "tp", axis=1, tiled=True)
    row_ids = joined * cand_dev + jnp.arange(cand_dev, dtype=jnp.int32)
    prefix_row = row_lookup(row_ids, prefix_ends)
    cand_pos = prefix_row + row_ids % CLEN
    prompt_pos = joined * prompt_dev + jnp.arange(prompt_dev, dtype=jnp.int32)
    key_value = jnp.concatenate([w_key, w_value], axis=1)
    if lax.axis_size("cache") == 2:
        other_half = lax.ppermute(key_value, "cache", [(0, 1), (1, 0)])
        key_value = jnp.where(
            lax.axis_index("cache") == 0,
            jnp.concatenate([key_value, other_half], axis=0),
            jnp.concatenate([other_half, key_value], axis=0),
        )
    else:
        key_value = lax.all_gather(key_value, "cache", axis=0, tiled=True)
    kv_prompt = jnp.dot(normed_p, key_value, preferred_element_type=jnp.float32)

    def keys_values(product, positions):
        rows = product.shape[0]
        keys = rotate(
            (product[:, :kv_width] + k_bias).reshape(rows, kv_local, head_size), positions
        ).astype(jnp.bfloat16)
        values = (product[:, kv_width:] + v_bias).astype(jnp.bfloat16)
        values = values.reshape(rows, kv_local, head_size)
        return jnp.concatenate([keys, values], axis=2).reshape(rows, 2 * kv_width)

    kv_p = lax.all_gather(
        keys_values(kv_prompt, prompt_pos), ("cache", "cand"), axis=0, tiled=True
    )
    q_cand = query_product(normed_c, w_query)
    kv_c = keys_values(jnp.dot(normed_c, key_value, preferred_element_type=jnp.float32), cand_pos)
    queries = rotate(
        (q_cand + q_bias).reshape(cand_dev, kv_local * groups, head_size), cand_pos
    ).astype(jnp.bfloat16)
    tile_rows = min(cand_dev, CLEN)
    tile_first = joined * cand_dev + tile_rows * jnp.arange(cand_dev // tile_rows, dtype=jnp.int32)
    prefixes = row_lookup(tile_first, prefix_ends)
    lengths = row_lookup(tile_first, cand_lengths)
    offsets = tile_first % CLEN
    if cand_dev < CLEN:
        kv_c = lax.all_gather(kv_c, ("cache", "cand"), axis=0, tiled=True)
        kv_c = lax.dynamic_slice_in_dim(kv_c, joined * cand_dev // CLEN * CLEN, CLEN)
    return attend(
        prefixes,
        lengths,
        offsets,
        queries.reshape(cand_dev, kv_local * groups * head_size),
        kv_p,
        kv_c,
        kv_local,
        groups,
    )


def solution(mesh):
    placed = (
        P(("cache", "cand"), None),
        P(("cache", "cand"), "tp"),
        P(),
        P("cache", "tp"),
        P("cache", "tp"),
        P("cache", "tp"),
        P("tp"),
        P("tp"),
        P("tp"),
        P(),
        P(),
    )
    return jax.shard_map(
        per_device,
        mesh=mesh,
        in_specs=placed,
        out_specs=P(("cache", "cand"), "tp"),
        check_vma=False,
    )
```
